32 devices in a mesh: groups: 2 (over x), pos: 8 (over z, y), mp: 2 (over core).
Axes of the slice: x: 2, y: 2, z: 4, core: 2. Of those that a mesh axis runs over, the one named last changes fastest.
Arguments:
- gate_stream: bfloat16 [8192, 4096], P(('groups', 'pos'), 'mp'), parts along dimension 0, may hold values from -6 to 6
- key_stream: bfloat16 [8192, 4096], P(('groups', 'pos'), 'mp'), parts along dimension 0, may hold values from -6 to 6
- value_stream: bfloat16 [8192, 4096], P(('groups', 'pos'), 'mp'), parts along dimension 0, may hold values from -6 to 6
- filters: float32 [4096, 128], P('mp')
- temps: float32 [32], P('mp'), may hold values from 4 to 24
- queries: bfloat16 [32, 256, 4096], P('groups', 'pos', 'mp'), parts along dimension 0, may hold values from -6 to 6
- blocks: int32 [32], P('groups'), parts along dimension 0, may hold values from 0 to 7, as said below
- sites: int32 [32], P('groups'), parts along dimension 0, may hold values from 128 to 4095, as said below
Outputs:
- hyena_out: bfloat16 [8192, 4096], P(('groups', 'pos'), 'mp'), parts along dimension 0
- attended: bfloat16 [32, 256, 4096], P('groups', 'pos', 'mp'), parts along dimension 0
The draws below stay inside these ranges and needn't reach their ends.
There are 2 independent parts, one for each index of `groups`. The reference program is written for one: setup_inputs(seed, part) draws one part's arguments, and reference() takes and returns one part's arrays. A program takes and returns all parts, laid end to end along the dimension named above; an argument that names none is the same for every part. Nothing has to cross between parts.
Inputs may be any that keep to these rules, and one draw needn't show every extreme that they name: `blocks`: A block is the 512 reference positions of one index of pos. Exactly one block is named by exactly 4 windows; every other block by at most two windows, and some block by exactly two. sites[w] - 512 * blocks[w] lies from 128 to 511.
All inputs are finite; a program needn't handle non-finite values.
Results may differ from the reference program's by a relative error of at most 0.01.
Values may be sent and summed in bfloat16 or wider, within the bound.
A program may use at most 128 MiB of HBM per device.

```python
import math
import jax
import jax.numpy as jnp
from jax import lax

HEADS = 32
HEAD_DIM = 128
CH = 4096
KLEN = 128
ROWS = 512
WLEN = 256
HOT = 4
WINDOWS = 16
REF = 4096


def shared_routing(key):
    base = jax.random.fold_in(key, 7)
    first, second, third = jax.random.split(base, 3)
    owners = WINDOWS // 2
    ranking = jax.random.permutation(first, WINDOWS).astype(jnp.int32)
    busiest = jax.random.randint(second, (), 0, owners).astype(jnp.int32)
    others = jax.random.permutation(third, owners - 1).astype(jnp.int32)
    others = others + (others >= busiest).astype(jnp.int32)
    position = jnp.clip(ranking - HOT, 0, WINDOWS - HOT - 1) % (owners - 1)
    return jnp.where(ranking < HOT, busiest, others[position]).astype(jnp.int32)


def draw_blocks(key, part):
    return shared_routing(key)


def draw_sites(key, part):
    chosen = shared_routing(key)
    offset = jax.random.randint(jax.random.fold_in(key, 11), (WINDOWS,), ROWS // 4, ROWS).astype(jnp.int32)
    return (chosen * ROWS + offset).astype(jnp.int32)


def draw_filters(key, part):
    first, second = jax.random.split(jax.random.fold_in(key, 3))
    life = jnp.exp(jax.random.uniform(first, (CH, 1), jnp.float32, math.log(30.0), math.log(4000.0)))
    raw = jnp.clip(jax.random.normal(second, (CH, KLEN), jnp.float32), -4.0, 4.0)
    ratio = jnp.exp(-1.0 / life)
    lags = jnp.arange(KLEN, dtype=jnp.float32)[None, :]
    decay = jnp.exp(-lags / life)
    total = (1.0 - ratio ** (2 * KLEN)) / (1.0 - ratio * ratio)
    return (raw * decay / jnp.sqrt(total)).astype(jnp.float32)


def levels(rng, shape, cuts, least, top_value):
    def one(dim, shards_of):
        draws = jax.random.uniform(jax.random.fold_in(jax.random.fold_in(rng, 6), dim), (shards_of,), jnp.float32, least / len(cuts), top_value / len(cuts))
        return jnp.repeat(jnp.exp(draws), shape[dim] // shards_of).reshape((-1,) + (1,) * (len(shape) - dim - 1))

    level = one(*cuts[0])
    for cut in cuts[1:]:
        level = level * one(*cut)
    return level


def centred(rng, extent, width, reach, cuts=(), held_as=jnp.bfloat16):
    array = jax.random.normal(rng, extent, jnp.float32) * width
    if len(cuts) > 0:
        array = levels(rng, extent, cuts, -0.22, 0.18) * array
    return jnp.clip(array, min=-reach, max=reach).astype(held_as)


def setup_inputs(seed: int = 0, part: int = 0) -> dict:
    seeds = jax.random.split(jax.random.key(seed), 9)
    part_splits = jax.random.split(jax.random.fold_in(seeds[8], part), 9)
    return {
        "gate_stream": centred(part_splits[0], (REF, CH), 1.0, 6.0, ((0, 8), (1, 2))),
        "key_stream": centred(part_splits[1], (REF, CH), 1.0, 6.0, ((0, 8), (1, 2))),
        "value_stream": centred(part_splits[2], (REF, CH), 1.0, 6.0, ((0, 8), (1, 2))),
        "filters": draw_filters(jax.random.fold_in(seeds[8], 71), part),
        "temps": jnp.clip(jnp.exp(math.log(24.0) - 1.7917595 * jax.random.uniform(seeds[4], (HEADS,), jnp.float32) ** levels(seeds[4], (HEADS,), ((0, 2),), -0.2, 0.2)), 4.0, 24.0),
        "queries": centred(part_splits[5], (WINDOWS, WLEN, CH), 1.0, 6.0, ((1, 8), (2, 2))),
        "blocks": draw_blocks(jax.random.fold_in(jax.random.fold_in(seeds[8], part), 71), part),
        "sites": draw_sites(jax.random.fold_in(jax.random.fold_in(seeds[8], part), 71), part),
    }


def widen(block):
    return lax.optimization_barrier(block).astype(jnp.float32)

def causal_mix(product, filters):
    taps = filters.shape[1]
    padded = jnp.concatenate([jnp.zeros((taps - 1, CH), jnp.bfloat16), product], 0)
    starts = (jnp.arange(REF // ROWS) * ROWS).astype(jnp.int32)

    def one_block(start):
        piece = widen(lax.dynamic_slice_in_dim(padded, start, ROWS + taps - 1, 0))

        def add_tap(step, total):
            shifted = lax.dynamic_slice_in_dim(piece, (taps - 1 - step).astype(jnp.int32), ROWS, 0)
            column = lax.dynamic_slice_in_dim(filters, step.astype(jnp.int32), 1, 1)[:, 0]
            return total + column[None, :] * shifted
        return lax.fori_loop(0, taps, add_tap, jnp.zeros((ROWS, CH), jnp.float32))
    return lax.map(one_block, starts).reshape(REF, CH)

def head_norm(block):
    shaped = widen(block).reshape(block.shape[:-1] + (HEADS, HEAD_DIM))
    scale = lax.rsqrt(lax.optimization_barrier(jnp.mean(shaped * shaped, axis=-1, keepdims=True)) + 1e-06)
    return (shaped * scale).reshape(block.shape).astype(jnp.bfloat16)

def attend(query_rows, key_rows, value_rows, offset, temps):
    qnorm = widen(head_norm(query_rows)).reshape(WLEN, HEADS, HEAD_DIM)
    keyed = widen(key_rows).reshape(ROWS, HEADS, HEAD_DIM)
    valued = widen(value_rows).reshape(ROWS, HEADS, HEAD_DIM)
    scores = jnp.einsum('qhd,khd->hqk', qnorm, keyed) * (temps / HEAD_DIM)[:, None, None]
    live = jnp.arange(ROWS)[None, None, :] < offset
    weights = jnp.where(live, jnp.exp(scores), 0.0)
    total = lax.optimization_barrier(jnp.sum(weights, axis=-1))
    numer = jnp.einsum('hqk,khd->qhd', widen(weights.astype(jnp.bfloat16)), valued)
    return (numer / total.T[:, :, None]).reshape(WLEN, CH).astype(jnp.bfloat16)

def reference(gate_stream, key_stream, value_stream, filters, temps, queries, blocks, sites):
    product = (key_stream.astype(jnp.float32) * value_stream.astype(jnp.float32)).astype(jnp.bfloat16)
    mixed = causal_mix(product, filters)
    hyena_out = (gate_stream.astype(jnp.float32) * mixed).astype(jnp.bfloat16)
    keys = head_norm(hyena_out)

    def one_window(item):
        query_rows, block, site = item
        start = (block * ROWS).astype(jnp.int32)
        key_rows = lax.dynamic_slice_in_dim(keys, start, ROWS, 0)
        value_rows = lax.dynamic_slice_in_dim(hyena_out, start, ROWS, 0)
        return attend(query_rows, key_rows, value_rows, site - block * ROWS, temps)
    attended = lax.map(one_window, (queries, blocks, sites))
    return (hyena_out, attended)
```

```python
import functools
import math

import jax
import jax.numpy as jnp
import numpy as np
from jax import lax
from jax.experimental import pallas as pl
from jax.experimental.pallas import tpu as pltpu
from jax.sharding import PartitionSpec as P

HEAD_DIM = 128
LOG2E = math.log2(math.e)


def transforms(taps):
    size = 2 * taps
    freq = (np.arange(taps) + 0.5) * (2 * np.pi / size)
    grid = freq[:, None] * np.arange(size)[None, :]
    both = np.concatenate([np.cos(grid), np.sin(grid)], 0)
    forward = both / size
    short = both[:, :taps] / taps
    inverse = both[:, taps:].T * taps * 2.0
    cast = lambda a: jnp.asarray(a, jnp.bfloat16)
    return cast(forward), cast(np.concatenate([short, short], 1)), cast(inverse)


def unit(block):
    return block * lax.rsqrt(jnp.mean(block * block, axis=-1, keepdims=True) + 1e-06)


def route_body(n, rows, blocks_ref, sites_ref, o_ref, seen):
    windows = blocks_ref.shape[0]
    me = lax.axis_index("pos")
    info = 2 * n + 2 + windows

    def clear(i, carry):
        o_ref[i] = 0
        return carry

    def fresh(i, carry):
        seen[i] = 0
        return carry

    def one(w, carry):
        block = blocks_ref[w]
        within = seen[block]
        seen[block] = within + 1
        place = jnp.where(within < 2, within * n + block, 2 * n + within - 2)
        o_ref[place] = w
        o_ref[2 * n + 2 + w] = place
        mine = block == me
        o_ref[info + within] = jnp.where(mine, sites_ref[w] - me * rows, o_ref[info + within])
        o_ref[info + 4] = jnp.where(mine & (within == 2), 1, o_ref[info + 4])
        return carry

    lax.fori_loop(0, 2 * n + 2, clear, 0)
    lax.fori_loop(0, n, fresh, 0)
    for slot in range(4):
        o_ref[info + slot] = rows
    o_ref[info + 4] = 0
    lax.fori_loop(0, windows, one, 0)


def route(blocks, sites, n, rows):
    windows = blocks.shape[0]
    smem = pl.BlockSpec(memory_space=pltpu.SMEM)
    return pl.pallas_call(
        functools.partial(route_body, n, rows),
        out_shape=jax.ShapeDtypeStruct((2 * n + windows + 7,), jnp.int32),
        in_specs=[smem, smem],
        out_specs=smem,
        scratch_shapes=[pltpu.SMEM((n,), jnp.int32)],
        name="route",
    )(blocks, sites)


def fused_body(
    n, inner, plan_ref, temps_ref, fwd_ref, short_ref, inv_ref, g_hbm, k_hbm, v_hbm, f_hbm,
    x_hbm, hyena_out, out_ref,
    gv, kv, vv, fv, qv, s0, s1, tail, halo, hy, keyed, q0, q1, qx, o0, o1, ox, acc, side, rise,
    fall, back,
    load, local, halo_sem, go_send, go_recv, ret_send, ret_recv, up_send, up_recv,
    down_send, down_recv, part_send, part_recv, rpart_send, rpart_recv,
    rup_send, rup_recv, rdown_send, rdown_recv,
):
    outer = n // inner
    me = lax.axis_index("pos")
    zi, yi = me // inner, me % inner
    rows, chans = gv.shape
    taps = fv.shape[1]
    toks = q0.shape[1]
    wide = 2 * HEAD_DIM
    windows = qv.shape[0]
    info = 2 * n + 2 + windows

    def remote(src, dst, send, recv, who):
        return pltpu.make_async_remote_copy(
            src_ref=src, dst_ref=dst, send_sem=send, recv_sem=recv,
            device_id={"pos": who}, device_id_type=pl.DeviceIdType.MESH,
        )

    loads = [
        pltpu.make_async_copy(src, dst, load.at[i])
        for i, (src, dst) in enumerate(
            ((k_hbm, kv), (v_hbm, vv), (x_hbm, qv), (g_hbm, gv), (f_hbm, fv))
        )
    ]
    for copy in loads:
        copy.start()

    def norm(slot, dst, at, first):
        w = plan_ref[slot]
        for h in range(chans // HEAD_DIM):
            cols = slice(h * HEAD_DIM, (h + 1) * HEAD_DIM)
            dst[at, first:first + toks, cols] = unit(
                qv[w, :, cols].astype(jnp.float32)
            ).astype(jnp.bfloat16)

    barrier = pltpu.get_barrier_semaphore()
    for off in range(1, n):
        pl.semaphore_signal(
            barrier, inc=1, device_id={"pos": (me + off) % n}, device_id_type=pl.DeviceIdType.MESH
        )
    pl.semaphore_wait(barrier, n - 1)

    loads[0].wait()
    loads[1].wait()
    at = slice(rows - taps, rows)
    tail[...] = (kv[at].astype(jnp.float32) * vv[at].astype(jnp.float32)).astype(jnp.bfloat16)
    halo_copy = remote(tail, halo, halo_sem.at[0], halo_sem.at[1], (me + 1) % n)

    loads[2].wait()
    norm(2 * n, qx, me, 0)
    norm(2 * n + 1, qx, me, toks)

    def across(z):
        slot = z * inner + yi
        return remote(
            qx.at[slot], qx.at[slot], part_send.at[z], part_recv.at[z], zi * inner + (inner - 1 - yi)
        )

    def upward(step):
        slot = jnp.maximum(zi - step + 1, 0) * inner + yi
        to = jnp.minimum(zi + 1, outer - 1) * inner + yi
        return remote(qx.at[slot], qx.at[slot], up_send.at[step], up_recv.at[step], to)

    def downward(step):
        slot = jnp.minimum(zi + step - 1, outer - 1) * inner + yi
        to = jnp.maximum(zi - 1, 0) * inner + yi
        return remote(qx.at[slot], qx.at[slot], down_send.at[step], down_recv.at[step], to)

    def gather_send(step):
        @pl.when((zi >= step - 1) & (zi < outer - 1))
        def _():
            upward(step).start()

        @pl.when((zi + step - 1 < outer) & (zi > 0))
        def _():
            downward(step).start()

        if inner == 2:
            @pl.when(zi >= step - 1)
            def _():
                across(jnp.maximum(zi - step + 1, 0)).start()

            if step > 1:
                @pl.when(zi + step - 1 < outer)
                def _():
                    across(jnp.minimum(zi + step - 1, outer - 1)).start()

    def gather_recv(step):
        @pl.when(zi >= step)
        def _():
            upward(step).wait_recv()

        @pl.when(zi + step < outer)
        def _():
            downward(step).wait_recv()

    def out_copy(slot, src, dst, off):
        to = (me + off) % n
        return remote(src.at[to], dst.at[me], go_send.at[slot, off], go_recv.at[slot, off], to)

    def back_copy(slot, src, off):
        to = (me + off) % n
        return remote(src.at[to], back.at[slot * n + me], ret_send.at[slot, off], ret_recv.at[slot, off], to)

    gather_send(1)

    def send(slot, buf, dst, low, high):
        def one(off, carry):
            to = (me + off) % n
            norm(slot * n + to, buf, to, 0)
            out_copy(slot, buf, dst, off).start()
            return carry

        lax.fori_loop(low, high, one, 0)

    hops = max(outer - 1, 1)
    cuts = [1 + (n - 1) * i // hops for i in range(hops + 1)]
    for step in range(hops):
        send(0, s0, q0, cuts[step], cuts[step + 1])
        if step == 0:
            @pl.when(me < n - 1)
            def _():
                halo_copy.start()

        if outer > 1:
            gather_recv(step + 1)
            gather_send(step + 2)
    send(1, s1, q1, 1, n)
    norm(me, q0, me, 0)
    norm(n + me, q1, me, 0)

    loads[3].wait()
    loads[4].wait()

    @pl.when(me > 0)
    def _():
        halo_copy.wait_recv()

    @pl.when(me == 0)
    def _():
        halo[...] = jnp.zeros_like(halo)

    def mix_tile(c, carry):
        cols = pl.ds(pl.multiple_of(c * wide, wide), wide)
        filt = fv[cols, :]
        high = filt.astype(jnp.bfloat16)
        low = (filt - high.astype(jnp.float32)).astype(jnp.bfloat16)
        fhat = lax.dot_general(
            short_ref[...], jnp.concatenate([high, low], 1), (((1,), (1,)), ((), ())),
            preferred_element_type=jnp.float32,
        )
        fc, fs = fhat[:taps], fhat[taps:]
        before = halo[:, cols]
        for b in range(rows // taps):
            here = slice(b * taps, (b + 1) * taps)
            z = (kv[here, cols].astype(jnp.float32) * vv[here, cols].astype(jnp.float32)).astype(jnp.bfloat16)
            zhat = jnp.dot(
                fwd_ref[...], jnp.concatenate([before, z], 0), preferred_element_type=jnp.float32
            )
            before = z
            zc, zs = zhat[:taps], zhat[taps:]
            prod = jnp.concatenate(
                [(fc * zc - fs * zs).astype(jnp.bfloat16), (fc * zs + fs * zc).astype(jnp.bfloat16)], 0
            )
            mixed = jnp.dot(inv_ref[...], prod, preferred_element_type=jnp.float32)
            out = (gv[here, cols].astype(jnp.float32) * mixed).astype(jnp.bfloat16)
            hy[here, cols] = out
            out = out.astype(jnp.float32)
            keyed[here, cols] = jnp.concatenate(
                [unit(out[:, :HEAD_DIM]), unit(out[:, HEAD_DIM:])], 1
            ).astype(jnp.bfloat16)
        return carry

    tiles = chans // wide
    lax.fori_loop(0, tiles, mix_tile, 0)
    hyena_copy = pltpu.make_async_copy(hy, hyena_out, local.at[2])
    hyena_copy.start()


    def attend(slot, q, o, first, hot):
        off = plan_ref[info + slot]
        seen = off * hot

        def one(c, carry):
            place = lax.broadcasted_iota(jnp.int32, (rows, HEAD_DIM), 0)
            ones = jnp.where(place < off, 1.0, 0.0).astype(jnp.bfloat16)
            live = jnp.where(place < seen, 1.0, 0.0).astype(jnp.bfloat16)
            for half in range(2):
                cols = pl.ds(pl.multiple_of(c * wide + half * HEAD_DIM, HEAD_DIM), HEAD_DIM)
                rows_q = q[:, pl.ds(first, toks), cols]
                if toks % 16:
                    rows_q = rows_q.astype(jnp.float32)
                rows_q = rows_q.reshape(n * toks, HEAD_DIM).astype(jnp.bfloat16)
                valued = jnp.concatenate([hy[:, cols] * live, ones], 1)
                scores = lax.dot_general(
                    rows_q, keyed[:, cols], (((1,), (1,)), ((), ())),
                    preferred_element_type=jnp.float32,
                )
                weights = jnp.exp2(scores * (temps_ref[c * 2 + half] * (LOG2E / HEAD_DIM)))
                numer = jnp.dot(
                    weights.astype(jnp.bfloat16), valued, preferred_element_type=jnp.float32
                )
                res = numer[:, :HEAD_DIM] / numer[:, HEAD_DIM:]
                o[:, pl.ds(first, toks), cols] = res.reshape(n, toks, HEAD_DIM).astype(jnp.bfloat16)
            return carry

        lax.fori_loop(0, tiles, one, 0)

    if inner == 2:
        for z in range(outer):
            across(z).wait_recv()
    hot = plan_ref[info + 4]
    attend(2, qx, ox, 0, hot)
    attend(3, qx, ox, toks, hot)

    def swap(z):
        return remote(
            ox.at[z * inner + (inner - 1 - yi)], side.at[z], rpart_send.at[z], rpart_recv.at[z],
            zi * inner + (inner - 1 - yi),
        )

    if inner == 2:
        for z in range(outer):
            swap(z).start()

    for off in range(1, n):
        out_copy(0, s0, q0, off).wait_recv()
    attend(0, q0, o0, 0, 1)
    mine0 = pltpu.make_async_copy(o0.at[me], back.at[me], local.at[0])
    mine0.start()

    def lift(z):
        to = jnp.minimum(zi + 1, outer - 1) * inner + yi
        return remote(acc.at[z], rise.at[z], rup_send.at[z], rup_recv.at[z], to)

    def drop(z):
        to = jnp.maximum(zi - 1, 0) * inner + yi
        return remote(acc.at[z], fall.at[z], rdown_send.at[z], rdown_recv.at[z], to)

    for z in range(outer):
        if inner == 2:
            swap(z).wait_recv()
            acc[z] = ox[z * inner + yi] + side[z]
        else:
            acc[z] = ox[z]

    def reduce_up(z):
        @pl.when(zi < z)
        def _():
            @pl.when(zi > 0)
            def _():
                lift(z).wait_recv()
                acc[z] = acc[z] + rise[z]

            lift(z).start()

    def reduce_down(z):
        @pl.when(zi > z)
        def _():
            @pl.when(zi < outer - 1)
            def _():
                drop(z).wait_recv()
                acc[z] = acc[z] + fall[z]

            drop(z).start()

    def reduce(step):
        if outer > 1:
            reduce_up(outer - 1 - step)
            reduce_down(step)

    reduce(0)
    for off in range(1, n):
        back_copy(0, o0, off).start()
    for off in range(1, n):
        out_copy(1, s1, q1, off).wait_recv()
    attend(1, q1, o1, 0, 1)
    mine1 = pltpu.make_async_copy(o1.at[me], back.at[n + me], local.at[1])
    mine1.start()
    rest = max(hops - 1, 1)
    cuts = [1 + (n - 1) * i // rest for i in range(rest + 1)]
    for step in range(rest):
        if step + 1 < hops:
            reduce(step + 1)
        for off in range(cuts[step], cuts[step + 1]):
            back_copy(1, o1, off).start()
    back[2 * n] = acc[zi, :toks]
    back[2 * n + 1] = acc[zi, toks:]

    def add(ref):
        back[2 * n] = back[2 * n] + ref[zi, :toks]
        back[2 * n + 1] = back[2 * n + 1] + ref[zi, toks:]

    @pl.when(zi > 0)
    def _():
        lift(zi).wait_recv()
        add(rise)

    @pl.when(zi < outer - 1)
    def _():
        drop(zi).wait_recv()
        add(fall)

    mine0.wait()
    mine1.wait()
    for off in range(1, n):
        back_copy(0, o0, off).wait_recv()
        back_copy(1, o1, off).wait_recv()

    def pick(w, carry):
        out_ref[w] = back[plan_ref[2 * n + 2 + w]]
        return carry

    lax.fori_loop(0, windows, pick, 0)

    for off in range(1, n):
        out_copy(0, s0, q0, off).wait_send()
        out_copy(1, s1, q1, off).wait_send()
        back_copy(0, o0, off).wait_send()
        back_copy(1, o1, off).wait_send()

    @pl.when(me < n - 1)
    def _():
        halo_copy.wait_send()

    for step in range(1, outer):
        @pl.when((zi >= step - 1) & (zi < outer - 1))
        def _(step=step):
            upward(step).wait_send()

        @pl.when((zi + step - 1 < outer) & (zi > 0))
        def _(step=step):
            downward(step).wait_send()

    for z in range(outer):
        if inner == 2:
            across(z).wait_send()
            swap(z).wait_send()

        @pl.when(zi < z)
        def _(z=z):
            lift(z).wait_send()

        @pl.when(zi > z)
        def _(z=z):
            drop(z).wait_send()

    hyena_copy.wait()


def fused(plan, temps, streams, filters, queries, n):
    gate, keys, values = streams
    rows, chans = gate.shape
    taps = filters.shape[1]
    windows, toks, _ = queries.shape
    inner = 2 if n % 2 == 0 else 1
    outer = n // inner
    half = jnp.bfloat16
    full = lambda *shape: pltpu.VMEM(shape, half)
    dma = lambda *shape: pltpu.SemaphoreType.DMA(shape)
    anywhere = pl.BlockSpec(memory_space=pl.ANY)
    return pl.pallas_call(
        functools.partial(fused_body, n, inner),
        out_shape=[
            jax.ShapeDtypeStruct((rows, chans), half),
            jax.ShapeDtypeStruct((windows, toks, chans), half),
        ],
        in_specs=[pl.BlockSpec(memory_space=pltpu.SMEM)] * 2
        + [pl.BlockSpec(memory_space=pltpu.VMEM)] * 3
        + [anywhere] * 5,
        out_specs=[anywhere, pl.BlockSpec(memory_space=pltpu.VMEM)],
        scratch_shapes=[
            full(rows, chans), full(rows, chans), full(rows, chans),
            pltpu.VMEM((chans, taps), jnp.float32),
            full(windows, toks, chans), full(n, toks, chans), full(n, toks, chans),
            full(taps, chans), full(taps, chans), full(rows, chans), full(rows, chans),
            full(n, toks, chans), full(n, toks, chans), full(n, 2 * toks, chans),
            full(n, toks, chans), full(n, toks, chans), full(n, 2 * toks, chans),
            full(outer, 2 * toks, chans), full(outer, 2 * toks, chans),
            full(outer, 2 * toks, chans), full(outer, 2 * toks, chans),
            full(2 * n + 2, toks, chans),
            dma(5), dma(3), dma(2), dma(2, n), dma(2, n), dma(2, n), dma(2, n),
            dma(outer + 1), dma(outer + 1), dma(outer + 1), dma(outer + 1),
            dma(outer), dma(outer), dma(outer), dma(outer),
            dma(outer), dma(outer), dma(outer), dma(outer),
        ],
        compiler_params=pltpu.CompilerParams(
            collective_id=0, has_side_effects=True, vmem_limit_bytes=67043328
        ),
        name="fused",
    )(plan, temps, *transforms(taps), gate, keys, values, filters, queries)


def hub_route_body(n, rows, blocks_ref, sites_ref, o_ref, seen):
    windows = blocks_ref.shape[0]
    me = lax.axis_index("pos")
    half = me // 4
    spots, offs = 2 * n + 2, 2 * n + 2 + windows
    hub = offs + 2 * n + 2

    def clear(i, carry):
        o_ref[i] = 0
        return carry

    def fresh(i, carry):
        seen[i] = 0
        return carry

    def one(w, carry):
        block = blocks_ref[w]
        within = seen[block]
        seen[block] = within + 1
        place = jnp.where(within < 2, within * n + block, 2 * n + within - 2)
        o_ref[place] = w
        o_ref[offs + place] = sites_ref[w] - block * rows
        z, column = block // 2, block % 2
        far = jnp.where(z // 2 == half, 0, 4)
        slot = jnp.where(within < 2, far + (z % 2) * 2 + within, 6 + within)
        o_ref[spots + w] = column * 10 + slot
        o_ref[hub] = jnp.where(within >= 2, z, o_ref[hub])
        return carry

    lax.fori_loop(0, hub + 1, clear, 0)
    lax.fori_loop(0, n, fresh, 0)
    lax.fori_loop(0, windows, one, 0)


def hub_route(blocks, sites, n, rows):
    windows = blocks.shape[0]
    smem = pl.BlockSpec(memory_space=pltpu.SMEM)
    return pl.pallas_call(
        functools.partial(hub_route_body, n, rows),
        out_shape=jax.ShapeDtypeStruct((4 * n + windows + 5,), jnp.int32),
        in_specs=[smem, smem],
        out_specs=smem,
        scratch_shapes=[pltpu.SMEM((n,), jnp.int32)],
        name="route",
    )(blocks, sites)


def hub_body(
    plan_ref, temps_ref, fwd_ref, short_ref, inv_ref, g_hbm, k_hbm, v_hbm, f_hbm, x_hbm,
    hyena_out, attended,
    kt, vt, gt, ft, qv, tail, halo, kv, qr, qs, ro, bk, cur, ot,
    load, x_sem, halo_send, halo_recv, kv_send, kv_recv, q_send, q_recv, r_send, r_recv,
    hy_sem, out_sem,
):
    n = 8
    tiles, rows, wide = kt.shape
    taps = ft.shape[2]
    windows, toks, _ = qv.shape
    me = lax.axis_index("pos")
    z, y = me // 2, me % 2
    half = z // 2
    hub_z = 1 + half
    end_z = 3 * half
    end = 1 - ((z + 1) // 2) % 2
    is_hub = z == hub_z
    is_end = z == end_z
    near, far = 2 * half, 2 * (1 - half)
    mate = 2 * z + 1 - y
    hub_own, hub_mate = 2 * hub_z + y, 2 * hub_z + 1 - y
    end_own, end_mate = 2 * end_z + y, 2 * end_z + 1 - y
    twin = 2 * (3 - hub_z) + y
    spots, offs = 2 * n + 2, 2 * n + 2 + windows

    def remote(src, dst, send, recv, who):
        return pltpu.make_async_remote_copy(
            src_ref=src, dst_ref=dst, send_sem=send, recv_sem=recv,
            device_id={"pos": who}, device_id_type=pl.DeviceIdType.MESH,
        )

    def columns(t):
        return pl.ds(pl.multiple_of(t * wide, wide), wide)

    def loads(t, which):
        pairs = (
            (k_hbm.at[:, columns(t)], kt), (v_hbm.at[:, columns(t)], vt),
            (f_hbm.at[columns(t), :], ft), (g_hbm.at[:, columns(t)], gt),
        )
        return [pltpu.make_async_copy(pairs[i][0], pairs[i][1].at[t], load.at[i, t]) for i in which]

    def load_start(t, carry):
        for copy in loads(t, range(4)):
            copy.start()
        return carry

    load_start(0, 0)
    x_copy = pltpu.make_async_copy(x_hbm, qv, x_sem)
    x_copy.start()
    lax.fori_loop(1, tiles, load_start, 0)

    barrier = pltpu.get_barrier_semaphore()
    for off in range(1, n):
        pl.semaphore_signal(
            barrier, inc=1, device_id={"pos": (me + off) % n}, device_id_type=pl.DeviceIdType.MESH
        )
    pl.semaphore_wait(barrier, n - 1)

    def halo_copy(t):
        return remote(tail.at[t], halo.at[t], halo_send.at[t], halo_recv.at[t], (me + 1) % n)

    def send_halo(t):
        for copy in loads(t, (0, 1)):
            copy.wait()
        at = slice(rows - taps, rows)
        tail[t] = (kt[t, at].astype(jnp.float32) * vt[t, at].astype(jnp.float32)).astype(jnp.bfloat16)

        @pl.when(me < n - 1)
        def _():
            halo_copy(t).start()

    send_halo(0)

    @pl.when(me == 0)
    def _():
        halo[...] = jnp.zeros_like(halo)

    def kv_copy(which, t):
        block, who = ((z, twin), (z, end_own), (end_z, twin), (z, hub_own))[which]
        return remote(kv.at[block, t], kv.at[block, t], kv_send.at[which % 3, t], kv_recv.at[block, t], who)

    def kv_wait(block, t):
        remote(kv.at[block, t], kv.at[block, t], kv_send.at[0, t], kv_recv.at[block, t], mate).wait_recv()

    def hyena_copy(t):
        return pltpu.make_async_copy(kv.at[z, t], hyena_out.at[:, columns(t)], hy_sem.at[t])

    def mix(t):
        for copy in loads(t, (2, 3)):
            copy.wait()
        filt = ft[t]
        high = filt.astype(jnp.bfloat16)
        low = (filt - high.astype(jnp.float32)).astype(jnp.bfloat16)
        fhat = lax.dot_general(
            short_ref[...], jnp.concatenate([high, low], 1), (((1,), (1,)), ((), ())),
            preferred_element_type=jnp.float32,
        )
        fc, fs = fhat[:taps], fhat[taps:]

        @pl.when(me > 0)
        def _():
            halo_copy(t).wait_recv()

        before = halo[t]
        for b in range(rows // taps):
            here = slice(b * taps, (b + 1) * taps)
            prod = (kt[t, here].astype(jnp.float32) * vt[t, here].astype(jnp.float32)).astype(jnp.bfloat16)
            zhat = jnp.dot(
                fwd_ref[...], jnp.concatenate([before, prod], 0), preferred_element_type=jnp.float32
            )
            before = prod
            zc, zs = zhat[:taps], zhat[taps:]
            both = jnp.concatenate(
                [(fc * zc - fs * zs).astype(jnp.bfloat16), (fc * zs + fs * zc).astype(jnp.bfloat16)], 0
            )
            mixed = jnp.dot(inv_ref[...], both, preferred_element_type=jnp.float32)
            kv[z, t, here] = (gt[t, here].astype(jnp.float32) * mixed).astype(jnp.bfloat16)

        @pl.when(is_hub)
        def _():
            kv_copy(0, t).start()
            kv_copy(1, t).start()

        @pl.when(is_end)
        def _():
            kv_copy(3, t).start()

        hyena_copy(t).start()

    def forward(t):
        kv_wait(end_z, t)
        kv_copy(2, t).start()

    def q_near(t):
        return remote(qs.at[t, 0:4], qr.at[t, 1, 0:4], q_send.at[0, t], q_recv.at[0, t], mate)

    def q_cross(t):
        at = 2 * end + 1
        return remote(qs.at[t, 4:10], qr.at[t, at, 4:10], q_send.at[1, t], q_recv.at[at, t], hub_mate)

    def q_along(t):
        return remote(qr.at[t, 0, 4:10], qr.at[t, 2, 4:10], q_send.at[2, t], q_recv.at[2, t], hub_own)

    def q_wait(src, t):
        remote(qr.at[t, 0, 4:10], qr.at[t, src, 4:10], q_send.at[0, t], q_recv.at[src, t], mate).wait_recv()

    def stage(t):
        for j in range(10):
            for own in range(2):
                column = y if own else 1 - y
                if j < 8:
                    block = 2 * ((near if j < 4 else far) + (j % 4) // 2) + column
                    w = plan_ref[(j % 2) * n + block]
                else:
                    w = plan_ref[2 * n + j - 8]
                for h in range(wide // HEAD_DIM):
                    cols = pl.ds(pl.multiple_of(t * wide + h * HEAD_DIM, HEAD_DIM), HEAD_DIM)
                    got = unit(qv[w, :, cols].astype(jnp.float32)).astype(jnp.bfloat16)
                    put = slice(h * HEAD_DIM, (h + 1) * HEAD_DIM)
                    if own:
                        qr[t, 0, j, :, put] = got
                    else:
                        qs[t, j, :, put] = got
        q_near(t).start()
        q_cross(t).start()

        @pl.when(is_end)
        def _():
            q_along(t).start()

    def attend(t, keyed, slots, offsets, sources):
        lane = lax.broadcasted_iota(jnp.int32, (1, rows), 1)
        many = sources * toks
        for h in range(wide // HEAD_DIM):
            cols = slice(h * HEAD_DIM, (h + 1) * HEAD_DIM)
            key = keyed(cols)
            power = lax.dot_general(
                jnp.ones((8, HEAD_DIM), jnp.bfloat16), key * key, (((1,), (1,)), ((), ())),
                preferred_element_type=jnp.float32,
            )[:1]
            scale = lax.rsqrt(power * (1.0 / HEAD_DIM) + 1e-06) * (
                temps_ref[t * (wide // HEAD_DIM) + h] * (LOG2E / HEAD_DIM)
            )
            query = jnp.concatenate(
                [qr[t, 0:sources, j, :, cols].reshape(many, HEAD_DIM) for j in slots], 0
            )
            scores = lax.dot_general(
                query, key, (((1,), (1,)), ((), ())), preferred_element_type=jnp.float32
            )
            raised = jnp.exp2(scores * scale)
            weights = jnp.concatenate(
                [
                    jnp.where(lane < off, raised[i * many:(i + 1) * many], 0.0).astype(jnp.bfloat16)
                    for i, off in enumerate(offsets)
                ], 0
            )
            numer = jnp.dot(
                weights, jnp.concatenate([key, jnp.ones((rows, HEAD_DIM), jnp.bfloat16)], 1),
                preferred_element_type=jnp.float32,
            )
            res = (numer[:, :HEAD_DIM] / numer[:, HEAD_DIM:]).astype(jnp.bfloat16)
            for i, j in enumerate(slots):
                for s in range(sources):
                    first = (i * sources + s) * toks
                    if s == 0:
                        bk[t, y * 10 + j, :, cols] = res[first:first + toks]
                    else:
                        ro[t, s - 1, j, :, cols] = res[first:first + toks]

    def offset(block_z, i):
        return plan_ref[offs + i * n + 2 * block_z + y]

    def attend_block(t, block_z, first, sources):
        attend(
            t, lambda cols: kv[block_z, t, :, cols], (first, first + 1),
            (offset(block_z, 0), offset(block_z, 1)), sources,
        )

    def r_near(t):
        return remote(
            ro.at[t, 0, 0:4], bk.at[t, pl.ds(y * 10, 4)], r_send.at[0, t], r_recv.at[0, t], mate
        )

    def r_wait(kind, column, t):
        at = bk.at[t, pl.ds(column * 10 + (0 if kind == 0 else 4), 4 if kind == 0 else 6)]
        remote(at, at, r_send.at[0, t], r_recv.at[kind, t], mate).wait_recv()

    def r_far(s, t):
        who, kind = ((mate, 1), (end_own, 1), (end_mate, 2))[s]
        return remote(
            ro.at[t, s, 4:10], bk.at[t, pl.ds(y * 10 + 4, 6)], r_send.at[1 + s, t],
            r_recv.at[kind, t], who,
        )

    def attend_near(t):
        q_near(t).wait_recv()

        @pl.when(is_end)
        def _():
            kv_wait(hub_z, t)

        attend_block(t, near, 0, 2)
        attend_block(t, near + 1, 2, 2)
        r_near(t).start()

    def attend_far(t):
        for src in range(1, 4):
            q_wait(src, t)
        kv_wait(3 - hub_z, t)
        kv_wait(3 - end_z, t)
        attend_block(t, far, 4, 4)
        attend_block(t, far + 1, 6, 4)
        hot = plan_ref[offs + 2 * n + 2]

        def hot_keys(cols):
            key = kv[0, t, :, cols]
            for block_z in range(1, 4):
                key = jnp.where(hot == block_z, kv[block_z, t, :, cols], key)
            return key

        attend(t, hot_keys, (8, 9), (plan_ref[offs + 2 * n], plan_ref[offs + 2 * n + 1]), 4)
        for s in range(3):
            r_far(s, t).start()

    def out_copy(t):
        return pltpu.make_async_copy(ot.at[t], attended.at[:, :, columns(t)], out_sem.at[t])

    def gather(t):
        r_wait(0, 1 - y, t)

        @pl.when(is_hub)
        def _():
            r_wait(1, 1 - y, t)

        @pl.when(is_end)
        def _():
            r_wait(1, y, t)
            r_wait(2, 1 - y, t)

        cur[...] = bk[t]

        def pick(w, carry):
            ot[t, w] = cur[plan_ref[spots + w]]
            return carry

        lax.fori_loop(0, windows, pick, 0)
        out_copy(t).start()

    def step(s, carry):
        @pl.when(s + 1 < tiles)
        def _():
            send_halo(s + 1)

        @pl.when(s < tiles)
        def _():
            mix(s)

            @pl.when(s == 0)
            def _():
                x_copy.wait()

            stage(s)

        @pl.when(is_hub & (s >= 1) & (s <= tiles))
        def _():
            forward(s - 1)

        @pl.when((s >= 2) & (s <= tiles + 1))
        def _():
            attend_near(s - 2)

            @pl.when(is_hub)
            def _():
                attend_far(s - 2)

        @pl.when(s >= 3)
        def _():
            gather(s - 3)

        return carry

    lax.fori_loop(0, tiles + 3, step, 0)

    def drain(t, carry):
        @pl.when(me < n - 1)
        def _():
            halo_copy(t).wait_send()

        q_near(t).wait_send()
        q_cross(t).wait_send()
        r_near(t).wait_send()

        @pl.when(is_hub)
        def _():
            for which in range(3):
                kv_copy(which, t).wait_send()
            for s in range(3):
                r_far(s, t).wait_send()

        @pl.when(is_end)
        def _():
            kv_copy(3, t).wait_send()
            q_along(t).wait_send()

        hyena_copy(t).wait()
        out_copy(t).wait()
        return carry

    lax.fori_loop(0, tiles, drain, 0)


def hub(plan, temps, streams, filters, queries):
    gate, keys, values = streams
    rows, chans = gate.shape
    taps = filters.shape[1]
    windows, toks, _ = queries.shape
    wide = 2 * HEAD_DIM
    tiles = chans // wide
    half = jnp.bfloat16
    full = lambda *shape: pltpu.VMEM(shape, half)
    dma = lambda *shape: pltpu.SemaphoreType.DMA(shape)
    anywhere = pl.BlockSpec(memory_space=pl.ANY)
    return pl.pallas_call(
        hub_body,
        out_shape=[
            jax.ShapeDtypeStruct((rows, chans), half),
            jax.ShapeDtypeStruct((windows, toks, chans), half),
        ],
        in_specs=[pl.BlockSpec(memory_space=pltpu.SMEM)] * 2
        + [pl.BlockSpec(memory_space=pltpu.VMEM)] * 3
        + [anywhere] * 5,
        out_specs=[anywhere, anywhere],
        scratch_shapes=[
            full(tiles, rows, wide), full(tiles, rows, wide), full(tiles, rows, wide),
            pltpu.VMEM((tiles, wide, taps), jnp.float32),
            full(windows, toks, chans), full(tiles, taps, wide), full(tiles, taps, wide),
            full(4, tiles, rows, wide),
            full(tiles, 4, 10, toks, wide), full(tiles, 10, toks, wide),
            full(tiles, 3, 10, toks, wide), full(tiles, 20, toks, wide),
            full(20, toks, wide), full(tiles, windows, toks, wide),
            dma(4, tiles), dma(), dma(tiles), dma(tiles), dma(3, tiles), dma(4, tiles),
            dma(3, tiles), dma(4, tiles), dma(4, tiles), dma(3, tiles), dma(tiles), dma(tiles),
        ],
        compiler_params=pltpu.CompilerParams(
            collective_id=1, has_side_effects=True, vmem_limit_bytes=60 * 1024 * 1024
        ),
        name="hub",
    )(plan, temps, *transforms(taps), gate, keys, values, filters, queries)


def shards(gate_stream, key_stream, value_stream, filters, temps, queries, blocks, sites):
    count = lax.axis_size("pos")
    streams = (gate_stream, key_stream, value_stream)
    if count == 8 and queries.shape[1] % 16 == 0:
        plan = hub_route(blocks, sites, count, gate_stream.shape[0])
        return tuple(hub(plan, temps, streams, filters, queries))
    plan = route(blocks, sites, count, gate_stream.shape[0])
    return tuple(
        fused(plan, temps, streams, filters, queries, count)
    )


def solution(mesh):
    placed = (
        P(("groups", "pos"), "mp"),
        P(("groups", "pos"), "mp"),
        P(("groups", "pos"), "mp"),
        P("mp", None),
        P("mp"),
        P("groups", "pos", "mp"),
        P("groups"),
        P("groups"),
    )
    return jax.shard_map(
        shards,
        mesh=mesh,
        in_specs=placed,
        out_specs=(P(("groups", "pos"), "mp"), P("groups", "pos", "mp")),
        check_vma=False,
    )
```

```python
import functools
import math

import jax
import jax.numpy as jnp
import numpy as np
from jax import lax
from jax.experimental import pallas as pl
from jax.experimental.pallas import tpu as pltpu
from jax.sharding import PartitionSpec as P

HEAD_DIM = 128
LOG2E = math.log2(math.e)


def transforms(taps):
    size = 2 * taps
    freq = (np.arange(taps) + 0.5) * (2 * np.pi / size)
    grid = freq[:, None] * np.arange(size)[None, :]
    both = np.concatenate([np.cos(grid), np.sin(grid)], 0)
    forward = both / size
    short = both[:, :taps] / taps
    inverse = both[:, taps:].T * taps * 2.0
    cast = lambda a: jnp.asarray(a, jnp.bfloat16)
    return cast(forward), cast(np.concatenate([short, short], 1)), cast(inverse)


def unit(block):
    return block * lax.rsqrt(jnp.mean(block * block, axis=-1, keepdims=True) + 1e-06)


def route_body(n, rows, blocks_ref, sites_ref, o_ref, seen):
    windows = blocks_ref.shape[0]
    me = lax.axis_index("pos")
    info = 2 * n + 2 + windows

    def clear(i, carry):
        o_ref[i] = 0
        return carry

    def fresh(i, carry):
        seen[i] = 0
        return carry

    def one(w, carry):
        block = blocks_ref[w]
        within = seen[block]
        seen[block] = within + 1
        place = jnp.where(within < 2, within * n + block, 2 * n + within - 2)
        o_ref[place] = w
        o_ref[2 * n + 2 + w] = place
        mine = block == me
        o_ref[info + within] = jnp.where(mine, sites_ref[w] - me * rows, o_ref[info + within])
        o_ref[info + 4] = jnp.where(mine & (within == 2), 1, o_ref[info + 4])
        return carry

    lax.fori_loop(0, 2 * n + 2, clear, 0)
    lax.fori_loop(0, n, fresh, 0)
    for slot in range(4):
        o_ref[info + slot] = rows
    o_ref[info + 4] = 0
    lax.fori_loop(0, windows, one, 0)


def route(blocks, sites, n, rows):
    windows = blocks.shape[0]
    smem = pl.BlockSpec(memory_space=pltpu.SMEM)
    return pl.pallas_call(
        functools.partial(route_body, n, rows),
        out_shape=jax.ShapeDtypeStruct((2 * n + windows + 7,), jnp.int32),
        in_specs=[smem, smem],
        out_specs=smem,
        scratch_shapes=[pltpu.SMEM((n,), jnp.int32)],
        name="route",
    )(blocks, sites)


def fused_body(
    n, inner, plan_ref, temps_ref, fwd_ref, short_ref, inv_ref, g_hbm, k_hbm, v_hbm, f_hbm,
    x_hbm, hyena_out, out_ref,
    gv, kv, vv, fv, qv, s0, s1, tail, halo, hy, keyed, q0, q1, qx, o0, o1, ox, acc, side, rise,
    fall, back,
    load, local, halo_sem, go_send, go_recv, ret_send, ret_recv, up_send, up_recv,
    down_send, down_recv, part_send, part_recv, rpart_send, rpart_recv,
    rup_send, rup_recv, rdown_send, rdown_recv,
):
    outer = n // inner
    me = lax.axis_index("pos")
    zi, yi = me // inner, me % inner
    rows, chans = gv.shape
    taps = fv.shape[1]
    toks = q0.shape[1]
    wide = 2 * HEAD_DIM
    windows = qv.shape[0]
    info = 2 * n + 2 + windows

    def remote(src, dst, send, recv, who):
        return pltpu.make_async_remote_copy(
            src_ref=src, dst_ref=dst, send_sem=send, recv_sem=recv,
            device_id={"pos": who}, device_id_type=pl.DeviceIdType.MESH,
        )

    loads = [
        pltpu.make_async_copy(src, dst, load.at[i])
        for i, (src, dst) in enumerate(
            ((k_hbm, kv), (v_hbm, vv), (x_hbm, qv), (g_hbm, gv), (f_hbm, fv))
        )
    ]
    for copy in loads:
        copy.start()

    def norm(slot, dst, at, first):
        w = plan_ref[slot]
        for h in range(chans // HEAD_DIM):
            cols = slice(h * HEAD_DIM, (h + 1) * HEAD_DIM)
            dst[at, first:first + toks, cols] = unit(
                qv[w, :, cols].astype(jnp.float32)
            ).astype(jnp.bfloat16)

    barrier = pltpu.get_barrier_semaphore()
    for off in range(1, n):
        pl.semaphore_signal(
            barrier, inc=1, device_id={"pos": (me + off) % n}, device_id_type=pl.DeviceIdType.MESH
        )
    pl.semaphore_wait(barrier, n - 1)

    loads[0].wait()
    loads[1].wait()
    at = slice(rows - taps, rows)
    tail[...] = (kv[at].astype(jnp.float32) * vv[at].astype(jnp.float32)).astype(jnp.bfloat16)
    halo_copy = remote(tail, halo, halo_sem.at[0], halo_sem.at[1], (me + 1) % n)

    loads[2].wait()
    norm(2 * n, qx, me, 0)
    norm(2 * n + 1, qx, me, toks)

    def across(z):
        slot = z * inner + yi
        return remote(
            qx.at[slot], qx.at[slot], part_send.at[z], part_recv.at[z], zi * inner + (inner - 1 - yi)
        )

    def upward(step):
        slot = jnp.maximum(zi - step + 1, 0) * inner + yi
        to = jnp.minimum(zi + 1, outer - 1) * inner + yi
        return remote(qx.at[slot], qx.at[slot], up_send.at[step], up_recv.at[step], to)

    def downward(step):
        slot = jnp.minimum(zi + step - 1, outer - 1) * inner + yi
        to = jnp.maximum(zi - 1, 0) * inner + yi
        return remote(qx.at[slot], qx.at[slot], down_send.at[step], down_recv.at[step], to)

    def gather_send(step):
        @pl.when((zi >= step - 1) & (zi < outer - 1))
        def _():
            upward(step).start()

        @pl.when((zi + step - 1 < outer) & (zi > 0))
        def _():
            downward(step).start()

        if inner == 2:
            @pl.when(zi >= step - 1)
            def _():
                across(jnp.maximum(zi - step + 1, 0)).start()

            if step > 1:
                @pl.when(zi + step - 1 < outer)
                def _():
                    across(jnp.minimum(zi + step - 1, outer - 1)).start()

    def gather_recv(step):
        @pl.when(zi >= step)
        def _():
            upward(step).wait_recv()

        @pl.when(zi + step < outer)
        def _():
            downward(step).wait_recv()

    def out_copy(slot, src, dst, off):
        to = (me + off) % n
        return remote(src.at[to], dst.at[me], go_send.at[slot, off], go_recv.at[slot, off], to)

    def back_copy(slot, src, off):
        to = (me + off) % n
        return remote(src.at[to], back.at[slot * n + me], ret_send.at[slot, off], ret_recv.at[slot, off], to)

    gather_send(1)

    def send(slot, buf, dst, low, high):
        def one(off, carry):
            to = (me + off) % n
            norm(slot * n + to, buf, to, 0)
            out_copy(slot, buf, dst, off).start()
            return carry

        lax.fori_loop(low, high, one, 0)

    hops = max(outer - 1, 1)
    cuts = [1 + (n - 1) * i // hops for i in range(hops + 1)]
    for step in range(hops):
        send(0, s0, q0, cuts[step], cuts[step + 1])
        if step == 0:
            @pl.when(me < n - 1)
            def _():
                halo_copy.start()

        if outer > 1:
            gather_recv(step + 1)
            gather_send(step + 2)
    send(1, s1, q1, 1, n)
    norm(me, q0, me, 0)
    norm(n + me, q1, me, 0)

    loads[3].wait()
    loads[4].wait()

    @pl.when(me > 0)
    def _():
        halo_copy.wait_recv()

    @pl.when(me == 0)
    def _():
        halo[...] = jnp.zeros_like(halo)

    def mix_tile(c, carry):
        cols = pl.ds(pl.multiple_of(c * wide, wide), wide)
        filt = fv[cols, :]
        high = filt.astype(jnp.bfloat16)
        low = (filt - high.astype(jnp.float32)).astype(jnp.bfloat16)
        fhat = lax.dot_general(
            short_ref[...], jnp.concatenate([high, low], 1), (((1,), (1,)), ((), ())),
            preferred_element_type=jnp.float32,
        )
        fc, fs = fhat[:taps], fhat[taps:]
        before = halo[:, cols]
        for b in range(rows // taps):
            here = slice(b * taps, (b + 1) * taps)
            z = (kv[here, cols].astype(jnp.float32) * vv[here, cols].astype(jnp.float32)).astype(jnp.bfloat16)
            zhat = jnp.dot(
                fwd_ref[...], jnp.concatenate([before, z], 0), preferred_element_type=jnp.float32
            )
            before = z
            zc, zs = zhat[:taps], zhat[taps:]
            prod = jnp.concatenate(
                [(fc * zc - fs * zs).astype(jnp.bfloat16), (fc * zs + fs * zc).astype(jnp.bfloat16)], 0
            )
            mixed = jnp.dot(inv_ref[...], prod, preferred_element_type=jnp.float32)
            out = (gv[here, cols].astype(jnp.float32) * mixed).astype(jnp.bfloat16)
            hy[here, cols] = out
            out = out.astype(jnp.float32)
            keyed[here, cols] = jnp.concatenate(
                [unit(out[:, :HEAD_DIM]), unit(out[:, HEAD_DIM:])], 1
            ).astype(jnp.bfloat16)
        return carry

    tiles = chans // wide
    lax.fori_loop(0, tiles, mix_tile, 0)
    hyena_copy = pltpu.make_async_copy(hy, hyena_out, local.at[2])
    hyena_copy.start()


    def attend(slot, q, o, first, hot):
        off = plan_ref[info + slot]
        seen = off * hot

        def one(c, carry):
            place = lax.broadcasted_iota(jnp.int32, (rows, HEAD_DIM), 0)
            ones = jnp.where(place < off, 1.0, 0.0).astype(jnp.bfloat16)
            live = jnp.where(place < seen, 1.0, 0.0).astype(jnp.bfloat16)
            for half in range(2):
                cols = pl.ds(pl.multiple_of(c * wide + half * HEAD_DIM, HEAD_DIM), HEAD_DIM)
                rows_q = q[:, pl.ds(first, toks), cols]
                if toks % 16:
                    rows_q = rows_q.astype(jnp.float32)
                rows_q = rows_q.reshape(n * toks, HEAD_DIM).astype(jnp.bfloat16)
                valued = jnp.concatenate([hy[:, cols] * live, ones], 1)
                scores = lax.dot_general(
                    rows_q, keyed[:, cols], (((1,), (1,)), ((), ())),
                    preferred_element_type=jnp.float32,
                )
                weights = jnp.exp2(scores * (temps_ref[c * 2 + half] * (LOG2E / HEAD_DIM)))
                numer = jnp.dot(
                    weights.astype(jnp.bfloat16), valued, preferred_element_type=jnp.float32
                )
                res = numer[:, :HEAD_DIM] / numer[:, HEAD_DIM:]
                o[:, pl.ds(first, toks), cols] = res.reshape(n, toks, HEAD_DIM).astype(jnp.bfloat16)
            return carry

        lax.fori_loop(0, tiles, one, 0)

    if inner == 2:
        for z in range(outer):
            across(z).wait_recv()
    hot = plan_ref[info + 4]
    attend(2, qx, ox, 0, hot)
    attend(3, qx, ox, toks, hot)

    def swap(z):
        return remote(
            ox.at[z * inner + (inner - 1 - yi)], side.at[z], rpart_send.at[z], rpart_recv.at[z],
            zi * inner + (inner - 1 - yi),
        )

    if inner == 2:
        for z in range(outer):
            swap(z).start()

    for off in range(1, n):
        out_copy(0, s0, q0, off).wait_recv()
    attend(0, q0, o0, 0, 1)
    mine0 = pltpu.make_async_copy(o0.at[me], back.at[me], local.at[0])
    mine0.start()

    def lift(z):
        to = jnp.minimum(zi + 1, outer - 1) * inner + yi
        return remote(acc.at[z], rise.at[z], rup_send.at[z], rup_recv.at[z], to)

    def drop(z):
        to = jnp.maximum(zi - 1, 0) * inner + yi
        return remote(acc.at[z], fall.at[z], rdown_send.at[z], rdown_recv.at[z], to)

    for z in range(outer):
        if inner == 2:
            swap(z).wait_recv()
            acc[z] = ox[z * inner + yi] + side[z]
        else:
            acc[z] = ox[z]

    def reduce_up(z):
        @pl.when(zi < z)
        def _():
            @pl.when(zi > 0)
            def _():
                lift(z).wait_recv()
                acc[z] = acc[z] + rise[z]

            lift(z).start()

    def reduce_down(z):
        @pl.when(zi > z)
        def _():
            @pl.when(zi < outer - 1)
            def _():
                drop(z).wait_recv()
                acc[z] = acc[z] + fall[z]

            drop(z).start()

    def reduce(step):
        if outer > 1:
            reduce_up(outer - 1 - step)
            reduce_down(step)

    reduce(0)
    for off in range(1, n):
        back_copy(0, o0, off).start()
    for off in range(1, n):
        out_copy(1, s1, q1, off).wait_recv()
    attend(1, q1, o1, 0, 1)
    mine1 = pltpu.make_async_copy(o1.at[me], back.at[n + me], local.at[1])
    mine1.start()
    rest = max(hops - 1, 1)
    cuts = [1 + (n - 1) * i // rest for i in range(rest + 1)]
    for step in range(rest):
        if step + 1 < hops:
            reduce(step + 1)
        for off in range(cuts[step], cuts[step + 1]):
            back_copy(1, o1, off).start()
    back[2 * n] = acc[zi, :toks]
    back[2 * n + 1] = acc[zi, toks:]

    def add(ref):
        back[2 * n] = back[2 * n] + ref[zi, :toks]
        back[2 * n + 1] = back[2 * n + 1] + ref[zi, toks:]

    @pl.when(zi > 0)
    def _():
        lift(zi).wait_recv()
        add(rise)

    @pl.when(zi < outer - 1)
    def _():
        drop(zi).wait_recv()
        add(fall)

    mine0.wait()
    mine1.wait()
    for off in range(1, n):
        back_copy(0, o0, off).wait_recv()
        back_copy(1, o1, off).wait_recv()

    def pick(w, carry):
        out_ref[w] = back[plan_ref[2 * n + 2 + w]]
        return carry

    lax.fori_loop(0, windows, pick, 0)

    for off in range(1, n):
        out_copy(0, s0, q0, off).wait_send()
        out_copy(1, s1, q1, off).wait_send()
        back_copy(0, o0, off).wait_send()
        back_copy(1, o1, off).wait_send()

    @pl.when(me < n - 1)
    def _():
        halo_copy.wait_send()

    for step in range(1, outer):
        @pl.when((zi >= step - 1) & (zi < outer - 1))
        def _(step=step):
            upward(step).wait_send()

        @pl.when((zi + step - 1 < outer) & (zi > 0))
        def _(step=step):
            downward(step).wait_send()

    for z in range(outer):
        if inner == 2:
            across(z).wait_send()
            swap(z).wait_send()

        @pl.when(zi < z)
        def _(z=z):
            lift(z).wait_send()

        @pl.when(zi > z)
        def _(z=z):
            drop(z).wait_send()

    hyena_copy.wait()


def fused(plan, temps, streams, filters, queries, n):
    gate, keys, values = streams
    rows, chans = gate.shape
    taps = filters.shape[1]
    windows, toks, _ = queries.shape
    inner = 2 if n % 2 == 0 else 1
    outer = n // inner
    half = jnp.bfloat16
    full = lambda *shape: pltpu.VMEM(shape, half)
    dma = lambda *shape: pltpu.SemaphoreType.DMA(shape)
    anywhere = pl.BlockSpec(memory_space=pl.ANY)
    return pl.pallas_call(
        functools.partial(fused_body, n, inner),
        out_shape=[
            jax.ShapeDtypeStruct((rows, chans), half),
            jax.ShapeDtypeStruct((windows, toks, chans), half),
        ],
        in_specs=[pl.BlockSpec(memory_space=pltpu.SMEM)] * 2
        + [pl.BlockSpec(memory_space=pltpu.VMEM)] * 3
        + [anywhere] * 5,
        out_specs=[anywhere, pl.BlockSpec(memory_space=pltpu.VMEM)],
        scratch_shapes=[
            full(rows, chans), full(rows, chans), full(rows, chans),
            pltpu.VMEM((chans, taps), jnp.float32),
            full(windows, toks, chans), full(n, toks, chans), full(n, toks, chans),
            full(taps, chans), full(taps, chans), full(rows, chans), full(rows, chans),
            full(n, toks, chans), full(n, toks, chans), full(n, 2 * toks, chans),
            full(n, toks, chans), full(n, toks, chans), full(n, 2 * toks, chans),
            full(outer, 2 * toks, chans), full(outer, 2 * toks, chans),
            full(outer, 2 * toks, chans), full(outer, 2 * toks, chans),
            full(2 * n + 2, toks, chans),
            dma(5), dma(3), dma(2), dma(2, n), dma(2, n), dma(2, n), dma(2, n),
            dma(outer + 1), dma(outer + 1), dma(outer + 1), dma(outer + 1),
            dma(outer), dma(outer), dma(outer), dma(outer),
            dma(outer), dma(outer), dma(outer), dma(outer),
        ],
        compiler_params=pltpu.CompilerParams(
            collective_id=0, has_side_effects=True, vmem_limit_bytes=67043328
        ),
        name="fused",
    )(plan, temps, *transforms(taps), gate, keys, values, filters, queries)


def hub_route_body(n, rows, blocks_ref, sites_ref, o_ref, seen):
    windows = blocks_ref.shape[0]
    me = lax.axis_index("pos")
    half = me // 4
    spots, offs = 2 * n + 2, 2 * n + 2 + windows
    hub = offs + 2 * n + 2

    def clear(i, carry):
        o_ref[i] = 0
        return carry

    def fresh(i, carry):
        seen[i] = 0
        return carry

    def one(w, carry):
        block = blocks_ref[w]
        within = seen[block]
        seen[block] = within + 1
        place = jnp.where(within < 2, within * n + block, 2 * n + within - 2)
        o_ref[place] = w
        o_ref[offs + place] = sites_ref[w] - block * rows
        z, column = block // 2, block % 2
        far = jnp.where(z // 2 == half, 0, 4)
        at_end = jnp.where((z == 0) | (z == 3), 2, 0)
        slot = jnp.where(within < 2, far + at_end + within, 6 + within)
        o_ref[spots + w] = column * 10 + slot
        o_ref[hub] = jnp.where(within >= 2, z, o_ref[hub])
        return carry

    lax.fori_loop(0, hub + 1, clear, 0)
    lax.fori_loop(0, n, fresh, 0)
    lax.fori_loop(0, windows, one, 0)


def hub_route(blocks, sites, n, rows):
    windows = blocks.shape[0]
    smem = pl.BlockSpec(memory_space=pltpu.SMEM)
    return pl.pallas_call(
        functools.partial(hub_route_body, n, rows),
        out_shape=jax.ShapeDtypeStruct((4 * n + windows + 5,), jnp.int32),
        in_specs=[smem, smem],
        out_specs=smem,
        scratch_shapes=[pltpu.SMEM((n,), jnp.int32)],
        name="route",
    )(blocks, sites)


def hub_body(
    plan_ref, temps_ref, fwd_ref, short_ref, inv_ref, g_hbm, k_hbm, v_hbm, f_hbm,
    x_hbm, hyena_out, attended,
    kt, vt, gt, ft, qv, tail, relay, halo, kv, qr, qs, ro, bk, cur,
    load, x_sem, halo_send, halo_recv, relay_send, relay_recv, kv_send, kv_recv, q_send, q_recv,
    r_send, r_recv, hy_sem,
):
    n = 8
    tiles, rows, wide = kt.shape
    taps = ft.shape[2]
    windows, toks, _ = qv.shape
    me = lax.axis_index("pos")
    z, y = me // 2, me % 2
    half = z // 2
    hub_z = 1 + half
    end_z = 3 * half
    is_hub = z == hub_z
    is_end = z == end_z
    mate = 2 * z + 1 - y
    hub_own, hub_mate = 2 * hub_z + y, 2 * hub_z + 1 - y
    end_own, end_mate = 2 * end_z + y, 2 * end_z + 1 - y
    twin = 2 * (3 - hub_z) + y
    spots, offs = 2 * n + 2, 2 * n + 2 + windows

    def remote(src, dst, send, recv, who):
        return pltpu.make_async_remote_copy(
            src_ref=src, dst_ref=dst, send_sem=send, recv_sem=recv,
            device_id={"pos": who}, device_id_type=pl.DeviceIdType.MESH,
        )

    def columns(t):
        return pl.ds(pl.multiple_of(t * wide, wide), wide)

    def loads(t, which):
        pairs = (
            (k_hbm.at[:, columns(t)], kt), (v_hbm.at[:, columns(t)], vt),
            (f_hbm.at[columns(t), :], ft), (g_hbm.at[:, columns(t)], gt),
        )
        return [pltpu.make_async_copy(pairs[i][0], pairs[i][1].at[t], load.at[i, t]) for i in which]

    def load_start(t, carry):
        for copy in loads(t, range(4)):
            copy.start()
        return carry

    load_start(0, 0)
    x_copy = pltpu.make_async_copy(x_hbm, qv, x_sem)
    x_copy.start()
    lax.fori_loop(1, tiles, load_start, 0)

    barrier = pltpu.get_barrier_semaphore()
    for off in range(1, n):
        pl.semaphore_signal(
            barrier, inc=1, device_id={"pos": (me + off) % n}, device_id_type=pl.DeviceIdType.MESH
        )
    pl.semaphore_wait(barrier, n - 1)

    def halo_copy(t):
        return remote(tail.at[t], halo.at[t], halo_send.at[t], halo_recv.at[t], (me + 1) % n)

    def relay_in(t):
        return remote(tail.at[t], relay.at[t], halo_send.at[t], relay_recv.at[t], mate)

    def relay_on(t):
        return remote(relay.at[t], halo.at[t], relay_send.at[t], halo_recv.at[t], (me + 2) % n)

    def detour(t):
        return (t >= 3) & (t != 4)

    def send_halo(t):
        for copy in loads(t, (0, 1)):
            copy.wait()
        at = slice(rows - taps, rows)
        tail[t] = (kt[t, at].astype(jnp.float32) * vt[t, at].astype(jnp.float32)).astype(jnp.bfloat16)

        @pl.when((y == 0) | ((me < n - 1) & ~detour(t)))
        def _():
            halo_copy(t).start()

        @pl.when((y == 1) & (me < n - 1) & detour(t))
        def _():
            relay_in(t).start()

    def pass_halo(t):
        @pl.when((y == 0) & (z < 3) & detour(t))
        def _():
            relay_in(t).wait_recv()
            relay_on(t).start()

    ahead = min(3, tiles)
    for t in range(ahead):
        send_halo(jnp.int32(t))

    @pl.when(me == 0)
    def _():
        halo[...] = jnp.zeros_like(halo)

    def kv_copy(which, t):
        block, who = ((z, twin), (z, end_own), (end_z, twin), (z, hub_own))[which]
        return remote(kv.at[block, t], kv.at[block, t], kv_send.at[which % 3, t], kv_recv.at[block, t], who)

    def kv_wait(block, t):
        remote(kv.at[block, t], kv.at[block, t], kv_send.at[0, t], kv_recv.at[block, t], mate).wait_recv()

    def hyena_copy(t):
        return pltpu.make_async_copy(kv.at[z, t], hyena_out.at[:, columns(t)], hy_sem.at[t])

    def mix(t):
        for copy in loads(t, (2, 3)):
            copy.wait()
        filt = ft[t]
        high = filt.astype(jnp.bfloat16)
        low = (filt - high.astype(jnp.float32)).astype(jnp.bfloat16)
        fhat = lax.dot_general(
            short_ref[...], jnp.concatenate([high, low], 1), (((1,), (1,)), ((), ())),
            preferred_element_type=jnp.float32,
        )
        fc, fs = fhat[:taps], fhat[taps:]

        def product(b):
            here = slice(b * taps, (b + 1) * taps)
            return (kt[t, here].astype(jnp.float32) * vt[t, here].astype(jnp.float32)).astype(jnp.bfloat16)

        def piece(b, before, prod):
            here = slice(b * taps, (b + 1) * taps)
            zhat = jnp.dot(
                fwd_ref[...], jnp.concatenate([before, prod], 0), preferred_element_type=jnp.float32
            )
            zc, zs = zhat[:taps], zhat[taps:]
            both = jnp.concatenate(
                [(fc * zc - fs * zs).astype(jnp.bfloat16), (fc * zs + fs * zc).astype(jnp.bfloat16)], 0
            )
            mixed = jnp.dot(inv_ref[...], both, preferred_element_type=jnp.float32)
            kv[z, t, here] = (gt[t, here].astype(jnp.float32) * mixed).astype(jnp.bfloat16)

        before = first = product(0)
        for b in range(1, rows // taps):
            prod = product(b)
            piece(b, before, prod)
            before = prod

        @pl.when(me > 0)
        def _():
            halo_copy(t).wait_recv()

        piece(0, halo[t], first)

        @pl.when(is_hub)
        def _():
            kv_copy(0, t).start()
            kv_copy(1, t).start()

        @pl.when(is_end)
        def _():
            kv_copy(3, t).start()

        hyena_copy(t).start()

    def forward(t):
        kv_wait(end_z, t)
        kv_copy(2, t).start()

    def q_near(t):
        return remote(qs.at[t], qr.at[t, 1], q_send.at[0, t], q_recv.at[0, t], mate)

    def q_along(t):
        return remote(
            qr.at[t, 0:2, 4:10], qr.at[t, 2:4, 4:10], q_send.at[1, t], q_recv.at[1, t], hub_own
        )

    def slot_z(j):
        return ((hub_z, end_z), (3 - hub_z, 3 - end_z))[j // 4][(j % 4) // 2]

    def stage(t):
        for j in range(10):
            for own in range(2):
                column = y if own else 1 - y
                if j < 8:
                    block = 2 * slot_z(j) + column
                    w = plan_ref[(j % 2) * n + block]
                else:
                    w = plan_ref[2 * n + j - 8]
                for h in range(wide // HEAD_DIM):
                    cols = pl.ds(pl.multiple_of(t * wide + h * HEAD_DIM, HEAD_DIM), HEAD_DIM)
                    got = unit(qv[w, :, cols].astype(jnp.float32)).astype(jnp.bfloat16)
                    put = slice(h * HEAD_DIM, (h + 1) * HEAD_DIM)
                    if own:
                        qr[t, 0, j, :, put] = got
                    else:
                        qs[t, j, :, put] = got
        q_near(t).start()

    def attend(t, keyed, slots, offsets, sources):
        lane = lax.broadcasted_iota(jnp.int32, (1, rows), 1)
        many = sources * toks
        for h in range(wide // HEAD_DIM):
            cols = slice(h * HEAD_DIM, (h + 1) * HEAD_DIM)
            key = keyed(cols)
            power = lax.dot_general(
                jnp.ones((8, HEAD_DIM), jnp.bfloat16), key * key, (((1,), (1,)), ((), ())),
                preferred_element_type=jnp.float32,
            )[:1]
            scale = lax.rsqrt(power * (1.0 / HEAD_DIM) + 1e-06) * (
                temps_ref[t * (wide // HEAD_DIM) + h] * (LOG2E / HEAD_DIM)
            )
            query = jnp.concatenate(
                [qr[t, 0:sources, j, :, cols].reshape(many, HEAD_DIM) for j in slots], 0
            )
            scores = lax.dot_general(
                query, key, (((1,), (1,)), ((), ())), preferred_element_type=jnp.float32
            )
            raised = jnp.exp2(scores * scale)
            weights = jnp.concatenate(
                [
                    jnp.where(lane < off, raised[i * many:(i + 1) * many], 0.0).astype(jnp.bfloat16)
                    for i, off in enumerate(offsets)
                ], 0
            )
            numer = jnp.dot(
                weights, jnp.concatenate([key, jnp.ones((rows, HEAD_DIM), jnp.bfloat16)], 1),
                preferred_element_type=jnp.float32,
            )
            res = (numer[:, :HEAD_DIM] / numer[:, HEAD_DIM:]).astype(jnp.bfloat16)
            for i, j in enumerate(slots):
                for s in range(sources):
                    first = (i * sources + s) * toks
                    if s == 0:
                        bk[t, y * 10 + j, :, cols] = res[first:first + toks]
                    else:
                        ro[t, s - 1, j, :, cols] = res[first:first + toks]

    def offset(block_z, i):
        return plan_ref[offs + i * n + 2 * block_z + y]

    def attend_block(t, block_z, first, sources):
        attend(
            t, lambda cols: kv[block_z, t, :, cols], (first, first + 1),
            (offset(block_z, 0), offset(block_z, 1)), sources,
        )

    def r_near(t):
        return remote(
            ro.at[t, 0, 0:4], bk.at[t, pl.ds(y * 10, 4)], r_send.at[0, t], r_recv.at[0, t], mate
        )

    def r_wait(kind, column, t):
        at = bk.at[t, pl.ds(column * 10 + (0 if kind == 0 else 4), 4 if kind == 0 else 6)]
        remote(at, at, r_send.at[0, t], r_recv.at[kind, t], mate).wait_recv()

    def r_far(s, t):
        who, kind = ((mate, 1), (end_own, 1), (end_mate, 2))[s]
        return remote(
            ro.at[t, s, 4:10], bk.at[t, pl.ds(y * 10 + 4, 6)], r_send.at[1 + s, t],
            r_recv.at[kind, t], who,
        )

    def attend_near(t):
        @pl.when(is_end)
        def _():
            kv_wait(hub_z, t)

        @pl.when(is_hub)
        def _():
            q_near(t).wait_recv()

        attend_block(t, hub_z, 0, 2)
        attend_block(t, end_z, 2, 2)
        r_near(t).start()

    def attend_far(t):
        q_along(t).wait_recv()
        kv_wait(3 - hub_z, t)
        attend_block(t, 3 - hub_z, 4, 4)
        kv_wait(3 - end_z, t)
        attend_block(t, 3 - end_z, 6, 4)
        hot = plan_ref[offs + 2 * n + 2]

        def hot_keys(cols):
            key = kv[0, t, :, cols]
            for block_z in range(1, 4):
                key = jnp.where(hot == block_z, kv[block_z, t, :, cols], key)
            return key

        attend(t, hot_keys, (8, 9), (plan_ref[offs + 2 * n], plan_ref[offs + 2 * n + 1]), 4)
        for s in range(3):
            r_far(s, t).start()

    def gather(t):
        r_wait(0, 1 - y, t)

        @pl.when(is_hub)
        def _():
            r_wait(1, 1 - y, t)

        @pl.when(is_end)
        def _():
            r_wait(1, y, t)
            r_wait(2, 1 - y, t)

        cur[...] = bk[t]

        def pick(w, carry):
            attended[w, :, columns(t)] = cur[plan_ref[spots + w]]
            return carry

        lax.fori_loop(0, windows, pick, 0)

    def step(s, carry):
        @pl.when(s + ahead < tiles)
        def _():
            send_halo(s + ahead)

        @pl.when(s < tiles)
        def _():
            mix(s)

            @pl.when(s == 0)
            def _():
                x_copy.wait()

            stage(s)

        @pl.when(s + ahead < tiles)
        def _():
            pass_halo(s + ahead)

        @pl.when((s >= 1) & (s <= tiles))
        def _():
            @pl.when(is_hub)
            def _():
                forward(s - 1)

            @pl.when(is_end)
            def _():
                q_near(s - 1).wait_recv()
                q_along(s - 1).start()

        @pl.when((s >= 2) & (s <= tiles + 1))
        def _():
            attend_near(s - 2)

            @pl.when(is_hub)
            def _():
                attend_far(s - 2)

        @pl.when(s >= 3)
        def _():
            gather(s - 3)

        return carry

    lax.fori_loop(0, tiles + 3, step, 0)

    def drain(t, carry):
        @pl.when(me < n - 1)
        def _():
            halo_copy(t).wait_send()

        @pl.when((y == 0) & (z < 3) & detour(t))
        def _():
            relay_on(t).wait_send()

        q_near(t).wait_send()
        r_near(t).wait_send()

        @pl.when(is_hub)
        def _():
            for which in range(3):
                kv_copy(which, t).wait_send()
            for s in range(3):
                r_far(s, t).wait_send()

        @pl.when(is_end)
        def _():
            kv_copy(3, t).wait_send()
            q_along(t).wait_send()

        hyena_copy(t).wait()
        return carry

    lax.fori_loop(0, tiles, drain, 0)


def settle_body(a_ref, b_ref, a_out, b_out, sems):
    copies = []
    for i, (src, dst) in enumerate(((a_ref, a_out), (b_ref, b_out))):
        part = src.shape[0] // 4
        for j in range(4):
            at = pl.ds(j * part, part)
            copies.append(pltpu.make_async_copy(src.at[at], dst.at[at], sems.at[i, j]))
    for copy in copies:
        copy.start()
    for copy in copies:
        copy.wait()


def settle(hyena, attended):
    anywhere = pl.BlockSpec(memory_space=pl.ANY)
    return pl.pallas_call(
        settle_body,
        out_shape=[jax.ShapeDtypeStruct(a.shape, a.dtype) for a in (hyena, attended)],
        in_specs=[pl.BlockSpec(memory_space=pltpu.VMEM)] * 2,
        out_specs=[anywhere] * 2,
        scratch_shapes=[pltpu.SemaphoreType.DMA((2, 4))],
        compiler_params=pltpu.CompilerParams(vmem_limit_bytes=16 * 1024 * 1024),
        name="settle",
    )(hyena, attended)


def hub(plan, temps, streams, filters, queries):
    gate, keys, values = streams
    rows, chans = gate.shape
    taps = filters.shape[1]
    windows, toks, _ = queries.shape
    wide = 2 * HEAD_DIM
    tiles = chans // wide
    half = jnp.bfloat16
    full = lambda *shape: pltpu.VMEM(shape, half)
    dma = lambda *shape: pltpu.SemaphoreType.DMA(shape)
    anywhere = pl.BlockSpec(memory_space=pl.ANY)
    return pl.pallas_call(
        hub_body,
        out_shape=[
            pltpu.VMEM((rows, chans), half),
            pltpu.VMEM((windows, toks, chans), half),
        ],
        in_specs=[pl.BlockSpec(memory_space=pltpu.SMEM)] * 2
        + [pl.BlockSpec(memory_space=pltpu.VMEM)] * 3
        + [anywhere] * 5,
        out_specs=[pl.BlockSpec(memory_space=pltpu.VMEM)] * 2,
        scratch_shapes=[
            full(tiles, rows, wide), full(tiles, rows, wide), full(tiles, rows, wide),
            pltpu.VMEM((tiles, wide, taps), jnp.float32),
            full(windows, toks, chans),
            full(tiles, taps, wide), full(tiles, taps, wide), full(tiles, taps, wide),
            full(4, tiles, rows, wide),
            full(tiles, 4, 10, toks, wide), full(tiles, 10, toks, wide),
            full(tiles, 3, 10, toks, wide), full(tiles, 20, toks, wide),
            full(20, toks, wide),
            dma(4, tiles), dma(), dma(tiles), dma(tiles), dma(tiles), dma(tiles),
            dma(3, tiles), dma(4, tiles), dma(2, tiles), dma(2, tiles),
            dma(4, tiles), dma(3, tiles), dma(tiles),
        ],
        compiler_params=pltpu.CompilerParams(
            collective_id=1, has_side_effects=True, vmem_limit_bytes=67043328 - 2 * chans * (rows + windows * toks)
        ),
        name="hub",
    )(plan, temps, *transforms(taps), gate, keys, values, filters, queries)


def shards(gate_stream, key_stream, value_stream, filters, temps, queries, blocks, sites):
    count = lax.axis_size("pos")
    streams = (gate_stream, key_stream, value_stream)
    if count == 8 and queries.shape[1] % 16 == 0:
        plan = hub_route(blocks, sites, count, gate_stream.shape[0])
        return tuple(settle(*hub(plan, temps, streams, filters, queries)))
    plan = route(blocks, sites, count, gate_stream.shape[0])
    return tuple(
        fused(plan, temps, streams, filters, queries, count)
    )


def solution(mesh):
    placed = (
        P(("groups", "pos"), "mp"),
        P(("groups", "pos"), "mp"),
        P(("groups", "pos"), "mp"),
        P("mp", None),
        P("mp"),
        P("groups", "pos", "mp"),
        P("groups"),
        P("groups"),
    )
    return jax.shard_map(
        shards,
        mesh=mesh,
        in_specs=placed,
        out_specs=(P(("groups", "pos"), "mp"), P("groups", "pos", "mp")),
        check_vma=False,
    )
```

```python
import functools
import math

import jax
import jax.numpy as jnp
import numpy as np
from jax import lax
from jax.experimental import pallas as pl
from jax.experimental.pallas import tpu as pltpu
from jax.sharding import PartitionSpec as P

HEAD_DIM = 128
LOG2E = math.log2(math.e)


def transforms(taps):
    size = 2 * taps
    freq = (np.arange(taps) + 0.5) * (2 * np.pi / size)
    grid = freq[:, None] * np.arange(size)[None, :]
    both = np.concatenate([np.cos(grid), np.sin(grid)], 0)
    forward = both / size
    short = both[:, :taps] / taps
    inverse = both[:, taps:].T * taps * 2.0
    cast = lambda a: jnp.asarray(a, jnp.bfloat16)
    return cast(forward), cast(np.concatenate([short, short], 1)), cast(inverse)


def unit(block):
    return block * lax.rsqrt(jnp.mean(block * block, axis=-1, keepdims=True) + 1e-06)


def route_body(n, rows, blocks_ref, sites_ref, o_ref, seen):
    windows = blocks_ref.shape[0]
    me = lax.axis_index("pos")
    info = 2 * n + 2 + windows

    def clear(i, carry):
        o_ref[i] = 0
        return carry

    def fresh(i, carry):
        seen[i] = 0
        return carry

    def one(w, carry):
        block = blocks_ref[w]
        within = seen[block]
        seen[block] = within + 1
        place = jnp.where(within < 2, within * n + block, 2 * n + within - 2)
        o_ref[place] = w
        o_ref[2 * n + 2 + w] = place
        mine = block == me
        o_ref[info + within] = jnp.where(mine, sites_ref[w] - me * rows, o_ref[info + within])
        o_ref[info + 4] = jnp.where(mine & (within == 2), 1, o_ref[info + 4])
        return carry

    lax.fori_loop(0, 2 * n + 2, clear, 0)
    lax.fori_loop(0, n, fresh, 0)
    for slot in range(4):
        o_ref[info + slot] = rows
    o_ref[info + 4] = 0
    lax.fori_loop(0, windows, one, 0)


def route(blocks, sites, n, rows):
    windows = blocks.shape[0]
    smem = pl.BlockSpec(memory_space=pltpu.SMEM)
    return pl.pallas_call(
        functools.partial(route_body, n, rows),
        out_shape=jax.ShapeDtypeStruct((2 * n + windows + 7,), jnp.int32),
        in_specs=[smem, smem],
        out_specs=smem,
        scratch_shapes=[pltpu.SMEM((n,), jnp.int32)],
        name="route",
    )(blocks, sites)


def fused_body(
    n, inner, plan_ref, temps_ref, fwd_ref, short_ref, inv_ref, g_hbm, k_hbm, v_hbm, f_hbm,
    x_hbm, hyena_out, out_ref,
    gv, kv, vv, fv, qv, s0, s1, tail, halo, hy, keyed, q0, q1, qx, o0, o1, ox, acc, side, rise,
    fall, back,
    load, local, halo_sem, go_send, go_recv, ret_send, ret_recv, up_send, up_recv,
    down_send, down_recv, part_send, part_recv, rpart_send, rpart_recv,
    rup_send, rup_recv, rdown_send, rdown_recv,
):
    outer = n // inner
    me = lax.axis_index("pos")
    zi, yi = me // inner, me % inner
    rows, chans = gv.shape
    taps = fv.shape[1]
    toks = q0.shape[1]
    wide = 2 * HEAD_DIM
    windows = qv.shape[0]
    info = 2 * n + 2 + windows

    def remote(src, dst, send, recv, who):
        return pltpu.make_async_remote_copy(
            src_ref=src, dst_ref=dst, send_sem=send, recv_sem=recv,
            device_id={"pos": who}, device_id_type=pl.DeviceIdType.MESH,
        )

    loads = [
        pltpu.make_async_copy(src, dst, load.at[i])
        for i, (src, dst) in enumerate(
            ((k_hbm, kv), (v_hbm, vv), (x_hbm, qv), (g_hbm, gv), (f_hbm, fv))
        )
    ]
    for copy in loads:
        copy.start()

    def norm(slot, dst, at, first):
        w = plan_ref[slot]
        for h in range(chans // HEAD_DIM):
            cols = slice(h * HEAD_DIM, (h + 1) * HEAD_DIM)
            dst[at, first:first + toks, cols] = unit(
                qv[w, :, cols].astype(jnp.float32)
            ).astype(jnp.bfloat16)

    barrier = pltpu.get_barrier_semaphore()
    for off in range(1, n):
        pl.semaphore_signal(
            barrier, inc=1, device_id={"pos": (me + off) % n}, device_id_type=pl.DeviceIdType.MESH
        )
    pl.semaphore_wait(barrier, n - 1)

    loads[0].wait()
    loads[1].wait()
    at = slice(rows - taps, rows)
    tail[...] = (kv[at].astype(jnp.float32) * vv[at].astype(jnp.float32)).astype(jnp.bfloat16)
    halo_copy = remote(tail, halo, halo_sem.at[0], halo_sem.at[1], (me + 1) % n)

    loads[2].wait()
    norm(2 * n, qx, me, 0)
    norm(2 * n + 1, qx, me, toks)

    def across(z):
        slot = z * inner + yi
        return remote(
            qx.at[slot], qx.at[slot], part_send.at[z], part_recv.at[z], zi * inner + (inner - 1 - yi)
        )

    def upward(step):
        slot = jnp.maximum(zi - step + 1, 0) * inner + yi
        to = jnp.minimum(zi + 1, outer - 1) * inner + yi
        return remote(qx.at[slot], qx.at[slot], up_send.at[step], up_recv.at[step], to)

    def downward(step):
        slot = jnp.minimum(zi + step - 1, outer - 1) * inner + yi
        to = jnp.maximum(zi - 1, 0) * inner + yi
        return remote(qx.at[slot], qx.at[slot], down_send.at[step], down_recv.at[step], to)

    def gather_send(step):
        @pl.when((zi >= step - 1) & (zi < outer - 1))
        def _():
            upward(step).start()

        @pl.when((zi + step - 1 < outer) & (zi > 0))
        def _():
            downward(step).start()

        if inner == 2:
            @pl.when(zi >= step - 1)
            def _():
                across(jnp.maximum(zi - step + 1, 0)).start()

            if step > 1:
                @pl.when(zi + step - 1 < outer)
                def _():
                    across(jnp.minimum(zi + step - 1, outer - 1)).start()

    def gather_recv(step):
        @pl.when(zi >= step)
        def _():
            upward(step).wait_recv()

        @pl.when(zi + step < outer)
        def _():
            downward(step).wait_recv()

    def out_copy(slot, src, dst, off):
        to = (me + off) % n
        return remote(src.at[to], dst.at[me], go_send.at[slot, off], go_recv.at[slot, off], to)

    def back_copy(slot, src, off):
        to = (me + off) % n
        return remote(src.at[to], back.at[slot * n + me], ret_send.at[slot, off], ret_recv.at[slot, off], to)

    gather_send(1)

    def send(slot, buf, dst, low, high):
        def one(off, carry):
            to = (me + off) % n
            norm(slot * n + to, buf, to, 0)
            out_copy(slot, buf, dst, off).start()
            return carry

        lax.fori_loop(low, high, one, 0)

    hops = max(outer - 1, 1)
    cuts = [1 + (n - 1) * i // hops for i in range(hops + 1)]
    for step in range(hops):
        send(0, s0, q0, cuts[step], cuts[step + 1])
        if step == 0:
            @pl.when(me < n - 1)
            def _():
                halo_copy.start()

        if outer > 1:
            gather_recv(step + 1)
            gather_send(step + 2)
    send(1, s1, q1, 1, n)
    norm(me, q0, me, 0)
    norm(n + me, q1, me, 0)

    loads[3].wait()
    loads[4].wait()

    @pl.when(me > 0)
    def _():
        halo_copy.wait_recv()

    @pl.when(me == 0)
    def _():
        halo[...] = jnp.zeros_like(halo)

    def mix_tile(c, carry):
        cols = pl.ds(pl.multiple_of(c * wide, wide), wide)
        filt = fv[cols, :]
        high = filt.astype(jnp.bfloat16)
        low = (filt - high.astype(jnp.float32)).astype(jnp.bfloat16)
        fhat = lax.dot_general(
            short_ref[...], jnp.concatenate([high, low], 1), (((1,), (1,)), ((), ())),
            preferred_element_type=jnp.float32,
        )
        fc, fs = fhat[:taps], fhat[taps:]
        before = halo[:, cols]
        for b in range(rows // taps):
            here = slice(b * taps, (b + 1) * taps)
            z = (kv[here, cols].astype(jnp.float32) * vv[here, cols].astype(jnp.float32)).astype(jnp.bfloat16)
            zhat = jnp.dot(
                fwd_ref[...], jnp.concatenate([before, z], 0), preferred_element_type=jnp.float32
            )
            before = z
            zc, zs = zhat[:taps], zhat[taps:]
            prod = jnp.concatenate(
                [(fc * zc - fs * zs).astype(jnp.bfloat16), (fc * zs + fs * zc).astype(jnp.bfloat16)], 0
            )
            mixed = jnp.dot(inv_ref[...], prod, preferred_element_type=jnp.float32)
            out = (gv[here, cols].astype(jnp.float32) * mixed).astype(jnp.bfloat16)
            hy[here, cols] = out
            out = out.astype(jnp.float32)
            keyed[here, cols] = jnp.concatenate(
                [unit(out[:, :HEAD_DIM]), unit(out[:, HEAD_DIM:])], 1
            ).astype(jnp.bfloat16)
        return carry

    tiles = chans // wide
    lax.fori_loop(0, tiles, mix_tile, 0)
    hyena_copy = pltpu.make_async_copy(hy, hyena_out, local.at[2])
    hyena_copy.start()


    def attend(slot, q, o, first, hot):
        off = plan_ref[info + slot]
        seen = off * hot

        def one(c, carry):
            place = lax.broadcasted_iota(jnp.int32, (rows, HEAD_DIM), 0)
            ones = jnp.where(place < off, 1.0, 0.0).astype(jnp.bfloat16)
            live = jnp.where(place < seen, 1.0, 0.0).astype(jnp.bfloat16)
            for half in range(2):
                cols = pl.ds(pl.multiple_of(c * wide + half * HEAD_DIM, HEAD_DIM), HEAD_DIM)
                rows_q = q[:, pl.ds(first, toks), cols]
                if toks % 16:
                    rows_q = rows_q.astype(jnp.float32)
                rows_q = rows_q.reshape(n * toks, HEAD_DIM).astype(jnp.bfloat16)
                valued = jnp.concatenate([hy[:, cols] * live, ones], 1)
                scores = lax.dot_general(
                    rows_q, keyed[:, cols], (((1,), (1,)), ((), ())),
                    preferred_element_type=jnp.float32,
                )
                weights = jnp.exp2(scores * (temps_ref[c * 2 + half] * (LOG2E / HEAD_DIM)))
                numer = jnp.dot(
                    weights.astype(jnp.bfloat16), valued, preferred_element_type=jnp.float32
                )
                res = numer[:, :HEAD_DIM] / numer[:, HEAD_DIM:]
                o[:, pl.ds(first, toks), cols] = res.reshape(n, toks, HEAD_DIM).astype(jnp.bfloat16)
            return carry

        lax.fori_loop(0, tiles, one, 0)

    if inner == 2:
        for z in range(outer):
            across(z).wait_recv()
    hot = plan_ref[info + 4]
    attend(2, qx, ox, 0, hot)
    attend(3, qx, ox, toks, hot)

    def swap(z):
        return remote(
            ox.at[z * inner + (inner - 1 - yi)], side.at[z], rpart_send.at[z], rpart_recv.at[z],
            zi * inner + (inner - 1 - yi),
        )

    if inner == 2:
        for z in range(outer):
            swap(z).start()

    for off in range(1, n):
        out_copy(0, s0, q0, off).wait_recv()
    attend(0, q0, o0, 0, 1)
    mine0 = pltpu.make_async_copy(o0.at[me], back.at[me], local.at[0])
    mine0.start()

    def lift(z):
        to = jnp.minimum(zi + 1, outer - 1) * inner + yi
        return remote(acc.at[z], rise.at[z], rup_send.at[z], rup_recv.at[z], to)

    def drop(z):
        to = jnp.maximum(zi - 1, 0) * inner + yi
        return remote(acc.at[z], fall.at[z], rdown_send.at[z], rdown_recv.at[z], to)

    for z in range(outer):
        if inner == 2:
            swap(z).wait_recv()
            acc[z] = ox[z * inner + yi] + side[z]
        else:
            acc[z] = ox[z]

    def reduce_up(z):
        @pl.when(zi < z)
        def _():
            @pl.when(zi > 0)
            def _():
                lift(z).wait_recv()
                acc[z] = acc[z] + rise[z]

            lift(z).start()

    def reduce_down(z):
        @pl.when(zi > z)
        def _():
            @pl.when(zi < outer - 1)
            def _():
                drop(z).wait_recv()
                acc[z] = acc[z] + fall[z]

            drop(z).start()

    def reduce(step):
        if outer > 1:
            reduce_up(outer - 1 - step)
            reduce_down(step)

    reduce(0)
    for off in range(1, n):
        back_copy(0, o0, off).start()
    for off in range(1, n):
        out_copy(1, s1, q1, off).wait_recv()
    attend(1, q1, o1, 0, 1)
    mine1 = pltpu.make_async_copy(o1.at[me], back.at[n + me], local.at[1])
    mine1.start()
    rest = max(hops - 1, 1)
    cuts = [1 + (n - 1) * i // rest for i in range(rest + 1)]
    for step in range(rest):
        if step + 1 < hops:
            reduce(step + 1)
        for off in range(cuts[step], cuts[step + 1]):
            back_copy(1, o1, off).start()
    back[2 * n] = acc[zi, :toks]
    back[2 * n + 1] = acc[zi, toks:]

    def add(ref):
        back[2 * n] = back[2 * n] + ref[zi, :toks]
        back[2 * n + 1] = back[2 * n + 1] + ref[zi, toks:]

    @pl.when(zi > 0)
    def _():
        lift(zi).wait_recv()
        add(rise)

    @pl.when(zi < outer - 1)
    def _():
        drop(zi).wait_recv()
        add(fall)

    mine0.wait()
    mine1.wait()
    for off in range(1, n):
        back_copy(0, o0, off).wait_recv()
        back_copy(1, o1, off).wait_recv()

    def pick(w, carry):
        out_ref[w] = back[plan_ref[2 * n + 2 + w]]
        return carry

    lax.fori_loop(0, windows, pick, 0)

    for off in range(1, n):
        out_copy(0, s0, q0, off).wait_send()
        out_copy(1, s1, q1, off).wait_send()
        back_copy(0, o0, off).wait_send()
        back_copy(1, o1, off).wait_send()

    @pl.when(me < n - 1)
    def _():
        halo_copy.wait_send()

    for step in range(1, outer):
        @pl.when((zi >= step - 1) & (zi < outer - 1))
        def _(step=step):
            upward(step).wait_send()

        @pl.when((zi + step - 1 < outer) & (zi > 0))
        def _(step=step):
            downward(step).wait_send()

    for z in range(outer):
        if inner == 2:
            across(z).wait_send()
            swap(z).wait_send()

        @pl.when(zi < z)
        def _(z=z):
            lift(z).wait_send()

        @pl.when(zi > z)
        def _(z=z):
            drop(z).wait_send()

    hyena_copy.wait()


def fused(plan, temps, streams, filters, queries, n):
    gate, keys, values = streams
    rows, chans = gate.shape
    taps = filters.shape[1]
    windows, toks, _ = queries.shape
    inner = 2 if n % 2 == 0 else 1
    outer = n // inner
    half = jnp.bfloat16
    full = lambda *shape: pltpu.VMEM(shape, half)
    dma = lambda *shape: pltpu.SemaphoreType.DMA(shape)
    anywhere = pl.BlockSpec(memory_space=pl.ANY)
    return pl.pallas_call(
        functools.partial(fused_body, n, inner),
        out_shape=[
            jax.ShapeDtypeStruct((rows, chans), half),
            jax.ShapeDtypeStruct((windows, toks, chans), half),
        ],
        in_specs=[pl.BlockSpec(memory_space=pltpu.SMEM)] * 2
        + [pl.BlockSpec(memory_space=pltpu.VMEM)] * 3
        + [anywhere] * 5,
        out_specs=[anywhere, pl.BlockSpec(memory_space=pltpu.VMEM)],
        scratch_shapes=[
            full(rows, chans), full(rows, chans), full(rows, chans),
            pltpu.VMEM((chans, taps), jnp.float32),
            full(windows, toks, chans), full(n, toks, chans), full(n, toks, chans),
            full(taps, chans), full(taps, chans), full(rows, chans), full(rows, chans),
            full(n, toks, chans), full(n, toks, chans), full(n, 2 * toks, chans),
            full(n, toks, chans), full(n, toks, chans), full(n, 2 * toks, chans),
            full(outer, 2 * toks, chans), full(outer, 2 * toks, chans),
            full(outer, 2 * toks, chans), full(outer, 2 * toks, chans),
            full(2 * n + 2, toks, chans),
            dma(5), dma(3), dma(2), dma(2, n), dma(2, n), dma(2, n), dma(2, n),
            dma(outer + 1), dma(outer + 1), dma(outer + 1), dma(outer + 1),
            dma(outer), dma(outer), dma(outer), dma(outer),
            dma(outer), dma(outer), dma(outer), dma(outer),
        ],
        compiler_params=pltpu.CompilerParams(
            collective_id=0, has_side_effects=True, vmem_limit_bytes=67043328
        ),
        name="fused",
    )(plan, temps, *transforms(taps), gate, keys, values, filters, queries)


def hub_route(n, rows, blocks_ref, sites_ref, plan_ref):
    windows = blocks_ref.shape[0]
    half = lax.axis_index("pos") // 4
    spots, offs = 2 * n + 2, 2 * n + 2 + windows
    blocks = [jnp.clip(blocks_ref[w], 0, n - 1) for w in range(windows)]
    places = []
    hot = jnp.int32(0)
    for w, block in enumerate(blocks):
        within = jnp.int32(0)
        for other in blocks[:w]:
            within = within + jnp.where(other == block, 1, 0)
        within = jnp.minimum(within, 3)
        places.append(jnp.where(within < 2, within * n + block, 2 * n + within - 2))
        z = lax.shift_right_logical(block, 1)
        far = jnp.where((z >= 2) == (half == 1), 0, 4)
        at_end = jnp.where((z == 0) | (z == 3), 2, 0)
        slot = jnp.where(within < 2, far + at_end + within, 6 + within)
        plan_ref[spots + w] = (block - 2 * z) * 10 + slot
        hot = jnp.where(within >= 2, z, hot)
    plan_ref[offs + 2 * n + 2] = hot
    reach = [sites_ref[w] - blocks[w] * rows for w in range(windows)]
    for p in range(2 * n + 2):
        w, off = jnp.int32(0), jnp.int32(0)
        for v in range(windows):
            hit = places[v] == p
            w = jnp.where(hit, v, w)
            off = jnp.where(hit, reach[v], off)
        plan_ref[p] = w
        plan_ref[offs + p] = off


def hub_body(
    blocks_ref, sites_ref, temps_ref, fwd_hbm, short_hbm, inv_hbm, g_hbm, k_hbm, v_hbm, f_hbm, x_hbm,
    hyena_out, attended,
    plan_ref, fwd_ref, short_ref, inv_ref, kt, vt, gt, ft, qv, tail, relay, halo, kv, qr, qs, ro, bk, cur,
    load, x_sem, halo_send, halo_recv, relay_send, relay_recv, kv_send, kv_recv, q_send, q_recv,
    r_send, r_recv, hy_sem, table_sem,
):
    n = 8
    tiles, rows, wide = kt.shape
    heads = wide // HEAD_DIM
    taps = ft.shape[2]
    windows, toks, _ = qv.shape
    me = lax.axis_index("pos")
    z, y = me // 2, me % 2
    half = z // 2
    hub_z = 1 + half
    end_z = 3 * half
    is_hub = z == hub_z
    is_end = z == end_z
    mate = 2 * z + 1 - y
    hub_own, hub_mate = 2 * hub_z + y, 2 * hub_z + 1 - y
    end_own, end_mate = 2 * end_z + y, 2 * end_z + 1 - y
    twin = 2 * (3 - hub_z) + y
    spots, offs = 2 * n + 2, 2 * n + 2 + windows

    def remote(src, dst, send, recv, who):
        return pltpu.make_async_remote_copy(
            src_ref=src, dst_ref=dst, send_sem=send, recv_sem=recv,
            device_id={"pos": who}, device_id_type=pl.DeviceIdType.MESH,
        )

    def columns(t):
        return pl.ds(pl.multiple_of(t * wide, wide), wide)

    def loads(t, which):
        pairs = (
            (k_hbm.at[:, columns(t)], kt), (v_hbm.at[:, columns(t)], vt),
            (f_hbm.at[columns(t), :], ft), (g_hbm.at[:, columns(t)], gt),
        )
        return [pltpu.make_async_copy(pairs[i][0], pairs[i][1].at[t], load.at[i, t]) for i in which]

    def load_start(t, carry):
        for copy in loads(t, range(4)):
            copy.start()
        return carry

    barrier = pltpu.get_barrier_semaphore()

    def greet(who):
        pl.semaphore_signal(
            barrier, inc=1, device_id={"pos": who}, device_id_type=pl.DeviceIdType.MESH
        )

    crosses = (me == 3) | (me == 4)
    for off in range(1, 4):
        greet(4 * half + (me + off) % 4)

    @pl.when(is_hub)
    def _():
        greet(twin)

    @pl.when(crosses)
    def _():
        greet(7 - me)

    tables = [
        pltpu.make_async_copy(src, dst, table_sem.at[i])
        for i, (src, dst) in enumerate(((short_hbm, short_ref), (fwd_hbm, fwd_ref), (inv_hbm, inv_ref)))
    ]
    for copy in tables:
        copy.start()
    load_start(0, 0)
    x_copy = pltpu.make_async_copy(x_hbm, qv, x_sem)
    x_copy.start()
    lax.fori_loop(1, tiles, load_start, 0)

    def halo_copy(t):
        return remote(tail.at[t], halo.at[t], halo_send.at[t], halo_recv.at[t], (me + 1) % n)

    def relay_in(t):
        return remote(tail.at[t], relay.at[t], halo_send.at[t], relay_recv.at[t], mate)

    def relay_on(t):
        return remote(relay.at[t], halo.at[t], relay_send.at[t], halo_recv.at[t], (me + 2) % n)

    def detour(t):
        return (t >= 3) & (t != 4)

    def make_halo(t):
        for copy in loads(t, (0, 1)):
            copy.wait()
        at = slice(rows - taps, rows)
        tail[t] = (kt[t, at].astype(jnp.float32) * vt[t, at].astype(jnp.float32)).astype(jnp.bfloat16)

    def send_halo(t):
        @pl.when((y == 0) | ((me < n - 1) & ~detour(t)))
        def _():
            halo_copy(t).start()

        @pl.when((y == 1) & (me < n - 1) & detour(t))
        def _():
            relay_in(t).start()

    def pass_halo(t):
        @pl.when((y == 0) & (z < 3) & detour(t))
        def _():
            relay_in(t).wait_recv()
            relay_on(t).start()

    whole = slice(0, rows)

    def kv_copy(which, t, h, at=whole):
        block, who = ((z, twin), (z, end_own), (end_z, twin), (z, hub_own))[which]
        part = kv.at[block, t, h, at]
        return remote(part, part, kv_send.at[which % 3, h, t], kv_recv.at[block, h, t], who)

    def kv_wait(block, t, h):
        part = kv.at[block, t, h]
        remote(part, part, kv_send.at[0, h, t], kv_recv.at[block, h, t], mate).wait_recv()

    def kv_start(t, at):
        @pl.when(is_hub)
        def _():
            for which in range(2):
                for h in range(heads):
                    kv_copy(which, t, h, at).start()

        @pl.when(is_end)
        def _():
            for h in range(heads):
                kv_copy(3, t, h, at).start()

    def hyena_copy(t, h):
        cols = pl.ds(pl.multiple_of(t * wide + h * HEAD_DIM, HEAD_DIM), HEAD_DIM)
        return pltpu.make_async_copy(kv.at[z, t, h], hyena_out.at[:, cols], hy_sem.at[h, t])

    def product(t, b):
        here = slice(b * taps, (b + 1) * taps)
        return (kt[t, here].astype(jnp.float32) * vt[t, here].astype(jnp.float32)).astype(jnp.bfloat16)

    def spectrum(t):
        filt = ft[t]
        high = filt.astype(jnp.bfloat16)
        low = (filt - high.astype(jnp.float32)).astype(jnp.bfloat16)
        fhat = lax.dot_general(
            short_ref[...], jnp.concatenate([high, low], 1), (((1,), (1,)), ((), ())),
            preferred_element_type=jnp.float32,
        )
        return fhat[:taps], fhat[taps:]

    def piece(t, b, before, prod, fc, fs):
        here = slice(b * taps, (b + 1) * taps)
        zhat = jnp.dot(
            fwd_ref[...], jnp.concatenate([before, prod], 0), preferred_element_type=jnp.float32
        )
        zc, zs = zhat[:taps], zhat[taps:]
        both = jnp.concatenate(
            [(fc * zc - fs * zs).astype(jnp.bfloat16), (fc * zs + fs * zc).astype(jnp.bfloat16)], 0
        )
        mixed = jnp.dot(inv_ref[...], both, preferred_element_type=jnp.float32)
        out = (gt[t, here].astype(jnp.float32) * mixed).astype(jnp.bfloat16)
        for h in range(heads):
            kv[z, t, h, here] = out[:, h * HEAD_DIM:(h + 1) * HEAD_DIM]

    def mix_late(t):
        for copy in loads(t, (2, 3)):
            copy.wait()
        fc, fs = spectrum(t)
        before = product(t, 0)
        for b in range(1, rows // taps):
            prod = product(t, b)
            piece(t, b, before, prod, fc, fs)
            before = prod
        return fc, fs

    def mix_early(t, fc, fs, split):
        if split:
            kv_start(t, slice(taps, rows))

        @pl.when(me > 0)
        def _():
            halo_copy(t).wait_recv()

        piece(t, 0, halo[t], product(t, 0), fc, fs)
        kv_start(t, slice(0, taps) if split else whole)
        for h in range(heads):
            hyena_copy(t, h).start()

    def forward(t):
        for h in range(heads):
            kv_wait(end_z, t, h)
            kv_copy(2, t, h).start()

    def q_near(t):
        return remote(qs.at[t], qr.at[t, 1], q_send.at[0, t], q_recv.at[0, t], mate)

    def q_along(t):
        return remote(
            qr.at[t, 0:2, 4:10], qr.at[t, 2:4, 4:10], q_send.at[1, t], q_recv.at[1, t], hub_own
        )

    def slot_z(j):
        return ((hub_z, end_z), (3 - hub_z, 3 - end_z))[j // 4][(j % 4) // 2]

    def stage(t):
        for j in range(10):
            for own in range(2):
                column = y if own else 1 - y
                if j < 8:
                    block = 2 * slot_z(j) + column
                    w = plan_ref[(j % 2) * n + block]
                else:
                    w = plan_ref[2 * n + j - 8]
                for h in range(wide // HEAD_DIM):
                    cols = pl.ds(pl.multiple_of(t * wide + h * HEAD_DIM, HEAD_DIM), HEAD_DIM)
                    got = unit(qv[w, :, cols].astype(jnp.float32)).astype(jnp.bfloat16)
                    put = slice(h * HEAD_DIM, (h + 1) * HEAD_DIM)
                    if own:
                        qr[t, 0, j, :, put] = got
                    else:
                        qs[t, j, :, put] = got
        q_near(t).start()

    def attend(t, h, key, slots, offsets, sources):
        lane = lax.broadcasted_iota(jnp.int32, (1, rows), 1)
        many = sources * toks
        cols = slice(h * HEAD_DIM, (h + 1) * HEAD_DIM)
        power = lax.dot_general(
            jnp.ones((8, HEAD_DIM), jnp.bfloat16), key * key, (((1,), (1,)), ((), ())),
            preferred_element_type=jnp.float32,
        )[:1]
        scale = lax.rsqrt(power * (1.0 / HEAD_DIM) + 1e-06) * (
            temps_ref[t * heads + h] * (LOG2E / HEAD_DIM)
        )
        query = jnp.concatenate(
            [qr[t, 0:sources, j, :, cols].reshape(many, HEAD_DIM) for j in slots], 0
        )
        scores = lax.dot_general(
            query, key, (((1,), (1,)), ((), ())), preferred_element_type=jnp.float32
        )
        raised = jnp.exp2(scores * scale)
        weights = jnp.concatenate(
            [
                jnp.where(lane < off, raised[i * many:(i + 1) * many], 0.0).astype(jnp.bfloat16)
                for i, off in enumerate(offsets)
            ], 0
        )
        numer = jnp.dot(
            weights, jnp.concatenate([key, jnp.ones((rows, HEAD_DIM), jnp.bfloat16)], 1),
            preferred_element_type=jnp.float32,
        )
        res = (numer[:, :HEAD_DIM] / numer[:, HEAD_DIM:]).astype(jnp.bfloat16)
        for i, j in enumerate(slots):
            for src in range(sources):
                first = (i * sources + src) * toks
                if src == 0:
                    bk[t, h, y * 10 + j] = res[first:first + toks]
                else:
                    ro[t, src - 1, h, j] = res[first:first + toks]

    def offset(block_z, i):
        return plan_ref[offs + i * n + 2 * block_z + y]

    def attend_block(t, h, block_z, first, sources):
        attend(
            t, h, kv[block_z, t, h], (first, first + 1),
            (offset(block_z, 0), offset(block_z, 1)), sources,
        )

    def r_near(t):
        return remote(
            ro.at[t, 0, :, 0:4], bk.at[t, :, pl.ds(y * 10, 4)], r_send.at[0, t], r_recv.at[0, t], mate
        )

    def r_early(src, t):
        who, kind = ((mate, 1), (end_own, 1), (end_mate, 2))[src]
        return remote(
            ro.at[t, src, :, 4:6], bk.at[t, :, pl.ds(y * 10 + 4, 2)], r_send.at[1 + src, t],
            r_recv.at[kind, t], who,
        )

    def r_late(src, t, h):
        who, kind = ((mate, 0), (end_own, 0), (end_mate, 1))[src]
        return remote(
            ro.at[t, src, h, 6:10], bk.at[t, h, pl.ds(y * 10 + 6, 4)], r_send.at[4 + 2 * src + h, t],
            r_recv.at[3 + 2 * kind + h, t], who,
        )

    def r_wait(part, sem, t):
        remote(part, part, r_send.at[0, t], r_recv.at[sem, t], mate).wait_recv()

    def r_wait_far(kind, column, t):
        r_wait(bk.at[t, :, pl.ds(column * 10 + 4, 2)], 1 + kind, t)
        for h in range(heads):
            r_wait(bk.at[t, h, pl.ds(column * 10 + 6, 4)], 3 + 2 * kind + h, t)

    def attend_near(t):
        @pl.when(is_end)
        def _():
            for h in range(heads):
                kv_wait(hub_z, t, h)

        @pl.when(is_hub)
        def _():
            q_near(t).wait_recv()

        for h in range(heads):
            attend_block(t, h, hub_z, 0, 2)
            attend_block(t, h, end_z, 2, 2)
        r_near(t).start()

    def attend_far(t):
        q_along(t).wait_recv()
        for h in range(heads):
            kv_wait(3 - hub_z, t, h)
            attend_block(t, h, 3 - hub_z, 4, 4)
        for src in range(3):
            r_early(src, t).start()
        hot = plan_ref[offs + 2 * n + 2]
        for h in range(heads):
            kv_wait(3 - end_z, t, h)
            attend_block(t, h, 3 - end_z, 6, 4)
            key = kv[0, t, h]
            for block_z in range(1, 4):
                key = jnp.where(hot == block_z, kv[block_z, t, h], key)
            attend(t, h, key, (8, 9), (plan_ref[offs + 2 * n], plan_ref[offs + 2 * n + 1]), 4)
            for src in range(3):
                r_late(src, t, h).start()

    def gather(t):
        r_wait(bk.at[t, :, pl.ds((1 - y) * 10, 4)], 0, t)

        @pl.when(is_hub)
        def _():
            r_wait_far(0, 1 - y, t)

        @pl.when(is_end)
        def _():
            r_wait_far(0, y, t)
            r_wait_far(1, 1 - y, t)

        cur[...] = bk[t]

        def pick(w, carry):
            for h in range(heads):
                cols = pl.ds(pl.multiple_of(t * wide + h * HEAD_DIM, HEAD_DIM), HEAD_DIM)
                attended[w, :, cols] = cur[h, plan_ref[spots + w]]
            return carry

        lax.fori_loop(0, windows, pick, 0)

    ahead = min(3, tiles)
    make_halo(jnp.int32(0))
    for copy in tables:
        copy.wait()
    fc, fs = mix_late(jnp.int32(0))
    for t in range(1, ahead):
        make_halo(jnp.int32(t))

    @pl.when(me == 0)
    def _():
        halo[...] = jnp.zeros_like(halo)

    pl.semaphore_wait(barrier, 3 + jnp.where(is_hub, 1, 0) + jnp.where(crosses, 1, 0))
    for t in range(ahead):
        send_halo(jnp.int32(t))
    mix_early(jnp.int32(0), fc, fs, True)
    hub_route(n, rows, blocks_ref, sites_ref, plan_ref)
    x_copy.wait()
    stage(jnp.int32(0))

    @pl.when(ahead < tiles)
    def _():
        make_halo(jnp.int32(min(ahead, tiles - 1)))
        send_halo(jnp.int32(min(ahead, tiles - 1)))
        pass_halo(jnp.int32(min(ahead, tiles - 1)))

    def step(s, carry):
        @pl.when(s + ahead < tiles)
        def _():
            make_halo(s + ahead)
            send_halo(s + ahead)

        @pl.when(s < tiles)
        def _():
            mix_early(s, *mix_late(s), False)
            stage(s)

        @pl.when(s + ahead < tiles)
        def _():
            pass_halo(s + ahead)

        @pl.when(s <= tiles)
        def _():
            @pl.when(is_hub)
            def _():
                forward(s - 1)

            @pl.when(is_end)
            def _():
                q_near(s - 1).wait_recv()
                q_along(s - 1).start()

        @pl.when((s >= 2) & (s <= tiles + 1))
        def _():
            attend_near(s - 2)

            @pl.when(is_hub)
            def _():
                attend_far(s - 2)

        @pl.when(s >= 3)
        def _():
            gather(s - 3)

        return carry

    lax.fori_loop(1, tiles + 3, step, 0)

    def drain(t, carry):
        @pl.when(me < n - 1)
        def _():
            halo_copy(t).wait_send()

        @pl.when((y == 0) & (z < 3) & detour(t))
        def _():
            relay_on(t).wait_send()

        q_near(t).wait_send()
        r_near(t).wait_send()

        @pl.when(is_hub)
        def _():
            for h in range(heads):
                for which in range(3):
                    kv_copy(which, t, h).wait_send()
                for src in range(3):
                    r_late(src, t, h).wait_send()
            for src in range(3):
                r_early(src, t).wait_send()

        @pl.when(is_end)
        def _():
            for h in range(heads):
                kv_copy(3, t, h).wait_send()
            q_along(t).wait_send()

        for h in range(heads):
            hyena_copy(t, h).wait()
        return carry

    lax.fori_loop(0, tiles, drain, 0)


def settle_body(a_ref, b_ref, a_out, b_out, sems):
    copies = []
    for i, (src, dst) in enumerate(((a_ref, a_out), (b_ref, b_out))):
        part = src.shape[0] // 4
        for j in range(4):
            at = pl.ds(j * part, part)
            copies.append(pltpu.make_async_copy(src.at[at], dst.at[at], sems.at[i, j]))
    for copy in copies:
        copy.start()
    for copy in copies:
        copy.wait()


def settle(hyena, attended):
    anywhere = pl.BlockSpec(memory_space=pl.ANY)
    return pl.pallas_call(
        settle_body,
        out_shape=[jax.ShapeDtypeStruct(a.shape, a.dtype) for a in (hyena, attended)],
        in_specs=[pl.BlockSpec(memory_space=pltpu.VMEM)] * 2,
        out_specs=[anywhere] * 2,
        scratch_shapes=[pltpu.SemaphoreType.DMA((2, 4))],
        compiler_params=pltpu.CompilerParams(vmem_limit_bytes=16 * 1024 * 1024),
        name="settle",
    )(hyena, attended)


def hub(blocks, sites, temps, streams, filters, queries):
    gate, keys, values = streams
    rows, chans = gate.shape
    taps = filters.shape[1]
    windows, toks, _ = queries.shape
    wide = 2 * HEAD_DIM
    tiles = chans // wide
    half = jnp.bfloat16
    full = lambda *shape: pltpu.VMEM(shape, half)
    dma = lambda *shape: pltpu.SemaphoreType.DMA(shape)
    anywhere = pl.BlockSpec(memory_space=pl.ANY)
    return pl.pallas_call(
        hub_body,
        out_shape=[
            pltpu.VMEM((rows, chans), half),
            pltpu.VMEM((windows, toks, chans), half),
        ],
        in_specs=[pl.BlockSpec(memory_space=pltpu.SMEM)] * 3
        + [anywhere] * 8,
        out_specs=[pl.BlockSpec(memory_space=pltpu.VMEM)] * 2,
        scratch_shapes=[
            pltpu.SMEM((64,), jnp.int32),
            full(2 * taps, 2 * taps), full(2 * taps, 2 * taps), full(taps, 2 * taps),
            full(tiles, rows, wide), full(tiles, rows, wide), full(tiles, rows, wide),
            pltpu.VMEM((tiles, wide, taps), jnp.float32),
            full(windows, toks, chans),
            full(tiles, taps, wide), full(tiles, taps, wide), full(tiles, taps, wide),
            full(4, tiles, 2, rows, HEAD_DIM),
            full(tiles, 4, 10, toks, wide), full(tiles, 10, toks, wide),
            full(tiles, 3, 2, 10, toks, HEAD_DIM), full(tiles, 2, 20, toks, HEAD_DIM),
            full(2, 20, toks, HEAD_DIM),
            dma(4, tiles), dma(), dma(tiles), dma(tiles), dma(tiles), dma(tiles),
            dma(3, 2, tiles), dma(4, 2, tiles), dma(2, tiles), dma(2, tiles),
            dma(10, tiles), dma(7, tiles), dma(2, tiles), dma(3),
        ],
        compiler_params=pltpu.CompilerParams(
            collective_id=1, has_side_effects=True, vmem_limit_bytes=67043328 - 2 * chans * (rows + windows * toks)
        ),
        name="hub",
    )(blocks, sites, temps, *transforms(taps), gate, keys, values, filters, queries)


def shards(gate_stream, key_stream, value_stream, filters, temps, queries, blocks, sites):
    count = lax.axis_size("pos")
    streams = (gate_stream, key_stream, value_stream)
    if count == 8 and queries.shape[1] % 16 == 0:
        return tuple(settle(*hub(blocks, sites, temps, streams, filters, queries)))
    plan = route(blocks, sites, count, gate_stream.shape[0])
    return tuple(
        fused(plan, temps, streams, filters, queries, count)
    )


def solution(mesh):
    placed = (
        P(("groups", "pos"), "mp"),
        P(("groups", "pos"), "mp"),
        P(("groups", "pos"), "mp"),
        P("mp", None),
        P("mp"),
        P("groups", "pos", "mp"),
        P("groups"),
        P("groups"),
    )
    return jax.shard_map(
        shards,
        mesh=mesh,
        in_specs=placed,
        out_specs=(P(("groups", "pos"), "mp"), P("groups", "pos", "mp")),
        check_vma=False,
    )
```

```python
import functools
import math

import jax
import jax.numpy as jnp
import numpy as np
from jax import lax
from jax.experimental import pallas as pl
from jax.experimental.pallas import tpu as pltpu
from jax.sharding import PartitionSpec as P

HEAD_DIM = 128
LOG2E = math.log2(math.e)


def transforms(taps):
    size = 2 * taps
    freq = (np.arange(taps) + 0.5) * (2 * np.pi / size)
    grid = freq[:, None] * np.arange(size)[None, :]
    both = np.concatenate([np.cos(grid), np.sin(grid)], 0)
    forward = both / size
    short = both[:, :taps] / taps
    inverse = both[:, taps:].T * taps * 2.0
    cast = lambda a: jnp.asarray(a, jnp.bfloat16)
    return cast(forward), cast(np.concatenate([short, short], 1)), cast(inverse)


def unit(block):
    return block * lax.rsqrt(jnp.mean(block * block, axis=-1, keepdims=True) + 1e-06)


def route_body(n, rows, blocks_ref, sites_ref, o_ref, seen):
    windows = blocks_ref.shape[0]
    me = lax.axis_index("pos")
    info = 2 * n + 2 + windows

    def clear(i, carry):
        o_ref[i] = 0
        return carry

    def fresh(i, carry):
        seen[i] = 0
        return carry

    def one(w, carry):
        block = blocks_ref[w]
        within = seen[block]
        seen[block] = within + 1
        place = jnp.where(within < 2, within * n + block, 2 * n + within - 2)
        o_ref[place] = w
        o_ref[2 * n + 2 + w] = place
        mine = block == me
        o_ref[info + within] = jnp.where(mine, sites_ref[w] - me * rows, o_ref[info + within])
        o_ref[info + 4] = jnp.where(mine & (within == 2), 1, o_ref[info + 4])
        return carry

    lax.fori_loop(0, 2 * n + 2, clear, 0)
    lax.fori_loop(0, n, fresh, 0)
    for slot in range(4):
        o_ref[info + slot] = rows
    o_ref[info + 4] = 0
    lax.fori_loop(0, windows, one, 0)


def route(blocks, sites, n, rows):
    windows = blocks.shape[0]
    smem = pl.BlockSpec(memory_space=pltpu.SMEM)
    return pl.pallas_call(
        functools.partial(route_body, n, rows),
        out_shape=jax.ShapeDtypeStruct((2 * n + windows + 7,), jnp.int32),
        in_specs=[smem, smem],
        out_specs=smem,
        scratch_shapes=[pltpu.SMEM((n,), jnp.int32)],
        name="route",
    )(blocks, sites)


def fused_body(
    n, inner, plan_ref, temps_ref, fwd_ref, short_ref, inv_ref, g_hbm, k_hbm, v_hbm, f_hbm,
    x_hbm, hyena_out, out_ref,
    gv, kv, vv, fv, qv, s0, s1, tail, halo, hy, keyed, q0, q1, qx, o0, o1, ox, acc, side, rise,
    fall, back,
    load, local, halo_sem, go_send, go_recv, ret_send, ret_recv, up_send, up_recv,
    down_send, down_recv, part_send, part_recv, rpart_send, rpart_recv,
    rup_send, rup_recv, rdown_send, rdown_recv,
):
    outer = n // inner
    me = lax.axis_index("pos")
    zi, yi = me // inner, me % inner
    rows, chans = gv.shape
    taps = fv.shape[1]
    toks = q0.shape[1]
    wide = 2 * HEAD_DIM
    windows = qv.shape[0]
    info = 2 * n + 2 + windows

    def remote(src, dst, send, recv, who):
        return pltpu.make_async_remote_copy(
            src_ref=src, dst_ref=dst, send_sem=send, recv_sem=recv,
            device_id={"pos": who}, device_id_type=pl.DeviceIdType.MESH,
        )

    loads = [
        pltpu.make_async_copy(src, dst, load.at[i])
        for i, (src, dst) in enumerate(
            ((k_hbm, kv), (v_hbm, vv), (x_hbm, qv), (g_hbm, gv), (f_hbm, fv))
        )
    ]
    for copy in loads:
        copy.start()

    def norm(slot, dst, at, first):
        w = plan_ref[slot]
        for h in range(chans // HEAD_DIM):
            cols = slice(h * HEAD_DIM, (h + 1) * HEAD_DIM)
            dst[at, first:first + toks, cols] = unit(
                qv[w, :, cols].astype(jnp.float32)
            ).astype(jnp.bfloat16)

    barrier = pltpu.get_barrier_semaphore()
    for off in range(1, n):
        pl.semaphore_signal(
            barrier, inc=1, device_id={"pos": (me + off) % n}, device_id_type=pl.DeviceIdType.MESH
        )
    pl.semaphore_wait(barrier, n - 1)

    loads[0].wait()
    loads[1].wait()
    at = slice(rows - taps, rows)
    tail[...] = (kv[at].astype(jnp.float32) * vv[at].astype(jnp.float32)).astype(jnp.bfloat16)
    halo_copy = remote(tail, halo, halo_sem.at[0], halo_sem.at[1], (me + 1) % n)

    loads[2].wait()
    norm(2 * n, qx, me, 0)
    norm(2 * n + 1, qx, me, toks)

    def across(z):
        slot = z * inner + yi
        return remote(
            qx.at[slot], qx.at[slot], part_send.at[z], part_recv.at[z], zi * inner + (inner - 1 - yi)
        )

    def upward(step):
        slot = jnp.maximum(zi - step + 1, 0) * inner + yi
        to = jnp.minimum(zi + 1, outer - 1) * inner + yi
        return remote(qx.at[slot], qx.at[slot], up_send.at[step], up_recv.at[step], to)

    def downward(step):
        slot = jnp.minimum(zi + step - 1, outer - 1) * inner + yi
        to = jnp.maximum(zi - 1, 0) * inner + yi
        return remote(qx.at[slot], qx.at[slot], down_send.at[step], down_recv.at[step], to)

    def gather_send(step):
        @pl.when((zi >= step - 1) & (zi < outer - 1))
        def _():
            upward(step).start()

        @pl.when((zi + step - 1 < outer) & (zi > 0))
        def _():
            downward(step).start()

        if inner == 2:
            @pl.when(zi >= step - 1)
            def _():
                across(jnp.maximum(zi - step + 1, 0)).start()

            if step > 1:
                @pl.when(zi + step - 1 < outer)
                def _():
                    across(jnp.minimum(zi + step - 1, outer - 1)).start()

    def gather_recv(step):
        @pl.when(zi >= step)
        def _():
            upward(step).wait_recv()

        @pl.when(zi + step < outer)
        def _():
            downward(step).wait_recv()

    def out_copy(slot, src, dst, off):
        to = (me + off) % n
        return remote(src.at[to], dst.at[me], go_send.at[slot, off], go_recv.at[slot, off], to)

    def back_copy(slot, src, off):
        to = (me + off) % n
        return remote(src.at[to], back.at[slot * n + me], ret_send.at[slot, off], ret_recv.at[slot, off], to)

    gather_send(1)

    def send(slot, buf, dst, low, high):
        def one(off, carry):
            to = (me + off) % n
            norm(slot * n + to, buf, to, 0)
            out_copy(slot, buf, dst, off).start()
            return carry

        lax.fori_loop(low, high, one, 0)

    hops = max(outer - 1, 1)
    cuts = [1 + (n - 1) * i // hops for i in range(hops + 1)]
    for step in range(hops):
        send(0, s0, q0, cuts[step], cuts[step + 1])
        if step == 0:
            @pl.when(me < n - 1)
            def _():
                halo_copy.start()

        if outer > 1:
            gather_recv(step + 1)
            gather_send(step + 2)
    send(1, s1, q1, 1, n)
    norm(me, q0, me, 0)
    norm(n + me, q1, me, 0)

    loads[3].wait()
    loads[4].wait()

    @pl.when(me > 0)
    def _():
        halo_copy.wait_recv()

    @pl.when(me == 0)
    def _():
        halo[...] = jnp.zeros_like(halo)

    def mix_tile(c, carry):
        cols = pl.ds(pl.multiple_of(c * wide, wide), wide)
        filt = fv[cols, :]
        high = filt.astype(jnp.bfloat16)
        low = (filt - high.astype(jnp.float32)).astype(jnp.bfloat16)
        fhat = lax.dot_general(
            short_ref[...], jnp.concatenate([high, low], 1), (((1,), (1,)), ((), ())),
            preferred_element_type=jnp.float32,
        )
        fc, fs = fhat[:taps], fhat[taps:]
        before = halo[:, cols]
        for b in range(rows // taps):
            here = slice(b * taps, (b + 1) * taps)
            z = (kv[here, cols].astype(jnp.float32) * vv[here, cols].astype(jnp.float32)).astype(jnp.bfloat16)
            zhat = jnp.dot(
                fwd_ref[...], jnp.concatenate([before, z], 0), preferred_element_type=jnp.float32
            )
            before = z
            zc, zs = zhat[:taps], zhat[taps:]
            prod = jnp.concatenate(
                [(fc * zc - fs * zs).astype(jnp.bfloat16), (fc * zs + fs * zc).astype(jnp.bfloat16)], 0
            )
            mixed = jnp.dot(inv_ref[...], prod, preferred_element_type=jnp.float32)
            out = (gv[here, cols].astype(jnp.float32) * mixed).astype(jnp.bfloat16)
            hy[here, cols] = out
            out = out.astype(jnp.float32)
            keyed[here, cols] = jnp.concatenate(
                [unit(out[:, :HEAD_DIM]), unit(out[:, HEAD_DIM:])], 1
            ).astype(jnp.bfloat16)
        return carry

    tiles = chans // wide
    lax.fori_loop(0, tiles, mix_tile, 0)
    hyena_copy = pltpu.make_async_copy(hy, hyena_out, local.at[2])
    hyena_copy.start()


    def attend(slot, q, o, first, hot):
        off = plan_ref[info + slot]
        seen = off * hot

        def one(c, carry):
            place = lax.broadcasted_iota(jnp.int32, (rows, HEAD_DIM), 0)
            ones = jnp.where(place < off, 1.0, 0.0).astype(jnp.bfloat16)
            live = jnp.where(place < seen, 1.0, 0.0).astype(jnp.bfloat16)
            for half in range(2):
                cols = pl.ds(pl.multiple_of(c * wide + half * HEAD_DIM, HEAD_DIM), HEAD_DIM)
                rows_q = q[:, pl.ds(first, toks), cols]
                if toks % 16:
                    rows_q = rows_q.astype(jnp.float32)
                rows_q = rows_q.reshape(n * toks, HEAD_DIM).astype(jnp.bfloat16)
                valued = jnp.concatenate([hy[:, cols] * live, ones], 1)
                scores = lax.dot_general(
                    rows_q, keyed[:, cols], (((1,), (1,)), ((), ())),
                    preferred_element_type=jnp.float32,
                )
                weights = jnp.exp2(scores * (temps_ref[c * 2 + half] * (LOG2E / HEAD_DIM)))
                numer = jnp.dot(
                    weights.astype(jnp.bfloat16), valued, preferred_element_type=jnp.float32
                )
                res = numer[:, :HEAD_DIM] / numer[:, HEAD_DIM:]
                o[:, pl.ds(first, toks), cols] = res.reshape(n, toks, HEAD_DIM).astype(jnp.bfloat16)
            return carry

        lax.fori_loop(0, tiles, one, 0)

    if inner == 2:
        for z in range(outer):
            across(z).wait_recv()
    hot = plan_ref[info + 4]
    attend(2, qx, ox, 0, hot)
    attend(3, qx, ox, toks, hot)

    def swap(z):
        return remote(
            ox.at[z * inner + (inner - 1 - yi)], side.at[z], rpart_send.at[z], rpart_recv.at[z],
            zi * inner + (inner - 1 - yi),
        )

    if inner == 2:
        for z in range(outer):
            swap(z).start()

    for off in range(1, n):
        out_copy(0, s0, q0, off).wait_recv()
    attend(0, q0, o0, 0, 1)
    mine0 = pltpu.make_async_copy(o0.at[me], back.at[me], local.at[0])
    mine0.start()

    def lift(z):
        to = jnp.minimum(zi + 1, outer - 1) * inner + yi
        return remote(acc.at[z], rise.at[z], rup_send.at[z], rup_recv.at[z], to)

    def drop(z):
        to = jnp.maximum(zi - 1, 0) * inner + yi
        return remote(acc.at[z], fall.at[z], rdown_send.at[z], rdown_recv.at[z], to)

    for z in range(outer):
        if inner == 2:
            swap(z).wait_recv()
            acc[z] = ox[z * inner + yi] + side[z]
        else:
            acc[z] = ox[z]

    def reduce_up(z):
        @pl.when(zi < z)
        def _():
            @pl.when(zi > 0)
            def _():
                lift(z).wait_recv()
                acc[z] = acc[z] + rise[z]

            lift(z).start()

    def reduce_down(z):
        @pl.when(zi > z)
        def _():
            @pl.when(zi < outer - 1)
            def _():
                drop(z).wait_recv()
                acc[z] = acc[z] + fall[z]

            drop(z).start()

    def reduce(step):
        if outer > 1:
            reduce_up(outer - 1 - step)
            reduce_down(step)

    reduce(0)
    for off in range(1, n):
        back_copy(0, o0, off).start()
    for off in range(1, n):
        out_copy(1, s1, q1, off).wait_recv()
    attend(1, q1, o1, 0, 1)
    mine1 = pltpu.make_async_copy(o1.at[me], back.at[n + me], local.at[1])
    mine1.start()
    rest = max(hops - 1, 1)
    cuts = [1 + (n - 1) * i // rest for i in range(rest + 1)]
    for step in range(rest):
        if step + 1 < hops:
            reduce(step + 1)
        for off in range(cuts[step], cuts[step + 1]):
            back_copy(1, o1, off).start()
    back[2 * n] = acc[zi, :toks]
    back[2 * n + 1] = acc[zi, toks:]

    def add(ref):
        back[2 * n] = back[2 * n] + ref[zi, :toks]
        back[2 * n + 1] = back[2 * n + 1] + ref[zi, toks:]

    @pl.when(zi > 0)
    def _():
        lift(zi).wait_recv()
        add(rise)

    @pl.when(zi < outer - 1)
    def _():
        drop(zi).wait_recv()
        add(fall)

    mine0.wait()
    mine1.wait()
    for off in range(1, n):
        back_copy(0, o0, off).wait_recv()
        back_copy(1, o1, off).wait_recv()

    def pick(w, carry):
        out_ref[w] = back[plan_ref[2 * n + 2 + w]]
        return carry

    lax.fori_loop(0, windows, pick, 0)

    for off in range(1, n):
        out_copy(0, s0, q0, off).wait_send()
        out_copy(1, s1, q1, off).wait_send()
        back_copy(0, o0, off).wait_send()
        back_copy(1, o1, off).wait_send()

    @pl.when(me < n - 1)
    def _():
        halo_copy.wait_send()

    for step in range(1, outer):
        @pl.when((zi >= step - 1) & (zi < outer - 1))
        def _(step=step):
            upward(step).wait_send()

        @pl.when((zi + step - 1 < outer) & (zi > 0))
        def _(step=step):
            downward(step).wait_send()

    for z in range(outer):
        if inner == 2:
            across(z).wait_send()
            swap(z).wait_send()

        @pl.when(zi < z)
        def _(z=z):
            lift(z).wait_send()

        @pl.when(zi > z)
        def _(z=z):
            drop(z).wait_send()

    hyena_copy.wait()


def fused(plan, temps, streams, filters, queries, n):
    gate, keys, values = streams
    rows, chans = gate.shape
    taps = filters.shape[1]
    windows, toks, _ = queries.shape
    inner = 2 if n % 2 == 0 else 1
    outer = n // inner
    half = jnp.bfloat16
    full = lambda *shape: pltpu.VMEM(shape, half)
    dma = lambda *shape: pltpu.SemaphoreType.DMA(shape)
    anywhere = pl.BlockSpec(memory_space=pl.ANY)
    return pl.pallas_call(
        functools.partial(fused_body, n, inner),
        out_shape=[
            jax.ShapeDtypeStruct((rows, chans), half),
            jax.ShapeDtypeStruct((windows, toks, chans), half),
        ],
        in_specs=[pl.BlockSpec(memory_space=pltpu.SMEM)] * 2
        + [pl.BlockSpec(memory_space=pltpu.VMEM)] * 3
        + [anywhere] * 5,
        out_specs=[anywhere, pl.BlockSpec(memory_space=pltpu.VMEM)],
        scratch_shapes=[
            full(rows, chans), full(rows, chans), full(rows, chans),
            pltpu.VMEM((chans, taps), jnp.float32),
            full(windows, toks, chans), full(n, toks, chans), full(n, toks, chans),
            full(taps, chans), full(taps, chans), full(rows, chans), full(rows, chans),
            full(n, toks, chans), full(n, toks, chans), full(n, 2 * toks, chans),
            full(n, toks, chans), full(n, toks, chans), full(n, 2 * toks, chans),
            full(outer, 2 * toks, chans), full(outer, 2 * toks, chans),
            full(outer, 2 * toks, chans), full(outer, 2 * toks, chans),
            full(2 * n + 2, toks, chans),
            dma(5), dma(3), dma(2), dma(2, n), dma(2, n), dma(2, n), dma(2, n),
            dma(outer + 1), dma(outer + 1), dma(outer + 1), dma(outer + 1),
            dma(outer), dma(outer), dma(outer), dma(outer),
            dma(outer), dma(outer), dma(outer), dma(outer),
        ],
        compiler_params=pltpu.CompilerParams(
            collective_id=0, has_side_effects=True, vmem_limit_bytes=67043328
        ),
        name="fused",
    )(plan, temps, *transforms(taps), gate, keys, values, filters, queries)


def hub_route(n, rows, blocks_ref, sites_ref, plan_ref):
    windows = blocks_ref.shape[0]
    half = lax.axis_index("pos") // 4
    spots, offs = 2 * n + 2, 2 * n + 2 + windows
    blocks = [jnp.clip(blocks_ref[w], 0, n - 1) for w in range(windows)]
    places = []
    hot = jnp.int32(0)
    for w, block in enumerate(blocks):
        within = jnp.int32(0)
        for other in blocks[:w]:
            within = within + jnp.where(other == block, 1, 0)
        within = jnp.minimum(within, 3)
        places.append(jnp.where(within < 2, within * n + block, 2 * n + within - 2))
        z = lax.shift_right_logical(block, 1)
        far = jnp.where((z >= 2) == (half == 1), 0, 4)
        at_end = jnp.where((z == 0) | (z == 3), 2, 0)
        slot = jnp.where(within < 2, far + at_end + within, 6 + within)
        plan_ref[spots + w] = (block - 2 * z) * 10 + slot
        hot = jnp.where(within >= 2, z, hot)
    plan_ref[offs + 2 * n + 2] = hot
    reach = [sites_ref[w] - blocks[w] * rows for w in range(windows)]
    for p in range(2 * n + 2):
        w, off = jnp.int32(0), jnp.int32(0)
        for v in range(windows):
            hit = places[v] == p
            w = jnp.where(hit, v, w)
            off = jnp.where(hit, reach[v], off)
        plan_ref[p] = w
        plan_ref[offs + p] = off


def hub_body(
    blocks_ref, sites_ref, temps_ref, fwd_hbm, short_hbm, inv_hbm, g_hbm, k_hbm, v_hbm, f_hbm, x_hbm,
    hyena_out, attended,
    plan_ref, fwd_ref, short_ref, inv_ref, kt, vt, gt, ft, qv, tail, relay, halo, kv, qr, qs, ro, bk, cur,
    load, x_sem, halo_send, halo_recv, relay_send, relay_recv, kv_send, kv_recv, q_send, q_recv,
    r_send, r_recv, hy_sem, table_sem,
):
    n = 8
    tiles, rows, wide = kt.shape
    heads = wide // HEAD_DIM
    taps = ft.shape[2]
    windows, toks, _ = qv.shape
    me = lax.axis_index("pos")
    z, y = me // 2, me % 2
    half = z // 2
    hub_z = 1 + half
    end_z = 3 * half
    is_hub = z == hub_z
    is_end = z == end_z
    mate = 2 * z + 1 - y
    hub_own, hub_mate = 2 * hub_z + y, 2 * hub_z + 1 - y
    end_own, end_mate = 2 * end_z + y, 2 * end_z + 1 - y
    twin = 2 * (3 - hub_z) + y
    spots, offs = 2 * n + 2, 2 * n + 2 + windows

    def remote(src, dst, send, recv, who):
        return pltpu.make_async_remote_copy(
            src_ref=src, dst_ref=dst, send_sem=send, recv_sem=recv,
            device_id={"pos": who}, device_id_type=pl.DeviceIdType.MESH,
        )

    def columns(t):
        return pl.ds(pl.multiple_of(t * wide, wide), wide)

    def loads(t, which):
        pairs = (
            (k_hbm.at[:, columns(t)], kt), (v_hbm.at[:, columns(t)], vt),
            (f_hbm.at[columns(t), :], ft), (g_hbm.at[:, columns(t)], gt),
        )
        return [pltpu.make_async_copy(pairs[i][0], pairs[i][1].at[t], load.at[i, t]) for i in which]

    def load_start(t, carry):
        for copy in loads(t, range(4)):
            copy.start()
        return carry

    barrier = pltpu.get_barrier_semaphore()

    def greet(who):
        pl.semaphore_signal(
            barrier, inc=1, device_id={"pos": who}, device_id_type=pl.DeviceIdType.MESH
        )

    crosses = (me == 3) | (me == 4)
    for off in range(1, 4):
        greet(4 * half + (me + off) % 4)

    @pl.when(is_hub)
    def _():
        greet(twin)

    @pl.when(crosses)
    def _():
        greet(7 - me)

    tables = [
        pltpu.make_async_copy(src, dst, table_sem.at[i])
        for i, (src, dst) in enumerate(((short_hbm, short_ref), (fwd_hbm, fwd_ref), (inv_hbm, inv_ref)))
    ]
    for copy in tables:
        copy.start()
    load_start(0, 0)
    x_copy = pltpu.make_async_copy(x_hbm, qv, x_sem)
    x_copy.start()
    lax.fori_loop(1, tiles, load_start, 0)

    def halo_copy(t):
        return remote(tail.at[t], halo.at[t], halo_send.at[t], halo_recv.at[t], (me + 1) % n)

    def relay_in(t):
        return remote(tail.at[t], relay.at[t], halo_send.at[t], relay_recv.at[t], mate)

    def relay_on(t):
        return remote(relay.at[t], halo.at[t], relay_send.at[t], halo_recv.at[t], (me + 2) % n)

    def detour(t):
        return t >= 4

    def make_halo(t):
        for copy in loads(t, (0, 1)):
            copy.wait()
        at = slice(rows - taps, rows)
        tail[t] = (kt[t, at].astype(jnp.float32) * vt[t, at].astype(jnp.float32)).astype(jnp.bfloat16)

    def send_halo(t):
        @pl.when((y == 0) | ((me < n - 1) & ~detour(t)))
        def _():
            halo_copy(t).start()

        @pl.when((y == 1) & (me < n - 1) & detour(t))
        def _():
            relay_in(t).start()

    def pass_halo(t):
        @pl.when((y == 0) & (z < 3) & detour(t))
        def _():
            relay_in(t).wait_recv()
            relay_on(t).start()

    whole = slice(0, rows)

    def kv_copy(which, t, h, at=whole):
        block, who = ((z, twin), (z, end_own), (end_z, twin), (z, hub_own))[which]
        part = kv.at[block, t, h, at]
        return remote(part, part, kv_send.at[which % 3, h, t], kv_recv.at[block, h, t], who)

    def kv_wait(block, t, h):
        part = kv.at[block, t, h]
        remote(part, part, kv_send.at[0, h, t], kv_recv.at[block, h, t], mate).wait_recv()

    def kv_start(t, at):
        @pl.when(is_hub)
        def _():
            for which in range(2):
                for h in range(heads):
                    kv_copy(which, t, h, at).start()

        @pl.when(is_end)
        def _():
            for h in range(heads):
                kv_copy(3, t, h, at).start()

    def hyena_copy(t, h):
        cols = pl.ds(pl.multiple_of(t * wide + h * HEAD_DIM, HEAD_DIM), HEAD_DIM)
        return pltpu.make_async_copy(kv.at[z, t, h], hyena_out.at[:, cols], hy_sem.at[h, t])

    def product(t, b):
        here = slice(b * taps, (b + 1) * taps)
        return (kt[t, here].astype(jnp.float32) * vt[t, here].astype(jnp.float32)).astype(jnp.bfloat16)

    def spectrum(t):
        filt = ft[t]
        high = filt.astype(jnp.bfloat16)
        low = (filt - high.astype(jnp.float32)).astype(jnp.bfloat16)
        fhat = lax.dot_general(
            short_ref[...], jnp.concatenate([high, low], 1), (((1,), (1,)), ((), ())),
            preferred_element_type=jnp.float32,
        )
        return fhat[:taps], fhat[taps:]

    def piece(t, b, before, prod, fc, fs):
        here = slice(b * taps, (b + 1) * taps)
        zhat = jnp.dot(
            fwd_ref[...], jnp.concatenate([before, prod], 0), preferred_element_type=jnp.float32
        )
        zc, zs = zhat[:taps], zhat[taps:]
        both = jnp.concatenate(
            [(fc * zc - fs * zs).astype(jnp.bfloat16), (fc * zs + fs * zc).astype(jnp.bfloat16)], 0
        )
        mixed = jnp.dot(inv_ref[...], both, preferred_element_type=jnp.float32)
        out = (gt[t, here].astype(jnp.float32) * mixed).astype(jnp.bfloat16)
        for h in range(heads):
            kv[z, t, h, here] = out[:, h * HEAD_DIM:(h + 1) * HEAD_DIM]

    def mix_late(t):
        for copy in loads(t, (2, 3)):
            copy.wait()
        fc, fs = spectrum(t)
        before = product(t, 0)
        for b in range(1, rows // taps):
            prod = product(t, b)
            piece(t, b, before, prod, fc, fs)
            before = prod
        return fc, fs

    def mix_early(t, fc, fs, split):
        if split:
            kv_start(t, slice(taps, rows))

        @pl.when(me > 0)
        def _():
            halo_copy(t).wait_recv()

        piece(t, 0, halo[t], product(t, 0), fc, fs)
        kv_start(t, slice(0, taps) if split else whole)
        for h in range(heads):
            hyena_copy(t, h).start()

    def forward(t):
        for h in range(heads):
            kv_wait(end_z, t, h)
            kv_copy(2, t, h).start()

    def q_near(t):
        return remote(qs.at[t], qr.at[t, 1], q_send.at[0, t], q_recv.at[0, t], mate)

    def q_along(t):
        return remote(
            qr.at[t, 0:2, 4:10], qr.at[t, 2:4, 4:10], q_send.at[1, t], q_recv.at[1, t], hub_own
        )

    def slot_z(j):
        return ((hub_z, end_z), (3 - hub_z, 3 - end_z))[j // 4][(j % 4) // 2]

    def stage(t):
        for j in range(10):
            for own in range(2):
                column = y if own else 1 - y
                if j < 8:
                    block = 2 * slot_z(j) + column
                    w = plan_ref[(j % 2) * n + block]
                else:
                    w = plan_ref[2 * n + j - 8]
                for h in range(wide // HEAD_DIM):
                    cols = pl.ds(pl.multiple_of(t * wide + h * HEAD_DIM, HEAD_DIM), HEAD_DIM)
                    got = unit(qv[w, :, cols].astype(jnp.float32)).astype(jnp.bfloat16)
                    put = slice(h * HEAD_DIM, (h + 1) * HEAD_DIM)
                    if own:
                        qr[t, 0, j, :, put] = got
                    else:
                        qs[t, j, :, put] = got
        q_near(t).start()

    def attend(t, h, key, slots, offsets, sources):
        lane = lax.broadcasted_iota(jnp.int32, (1, rows), 1)
        many = sources * toks
        cols = slice(h * HEAD_DIM, (h + 1) * HEAD_DIM)
        power = lax.dot_general(
            jnp.ones((8, HEAD_DIM), jnp.bfloat16), key * key, (((1,), (1,)), ((), ())),
            preferred_element_type=jnp.float32,
        )[:1]
        scale = lax.rsqrt(power * (1.0 / HEAD_DIM) + 1e-06) * (
            temps_ref[t * heads + h] * (LOG2E / HEAD_DIM)
        )
        query = jnp.concatenate(
            [qr[t, 0:sources, j, :, cols].reshape(many, HEAD_DIM) for j in slots], 0
        )
        scores = lax.dot_general(
            query, key, (((1,), (1,)), ((), ())), preferred_element_type=jnp.float32
        )
        raised = jnp.exp2(scores * scale)
        weights = jnp.concatenate(
            [
                jnp.where(lane < off, raised[i * many:(i + 1) * many], 0.0).astype(jnp.bfloat16)
                for i, off in enumerate(offsets)
            ], 0
        )
        numer = jnp.dot(
            weights, jnp.concatenate([key, jnp.ones((rows, HEAD_DIM), jnp.bfloat16)], 1),
            preferred_element_type=jnp.float32,
        )
        res = (numer[:, :HEAD_DIM] / numer[:, HEAD_DIM:]).astype(jnp.bfloat16)
        for i, j in enumerate(slots):
            for src in range(sources):
                first = (i * sources + src) * toks
                if src == 0:
                    bk[t, h, y * 10 + j] = res[first:first + toks]
                else:
                    ro[t, src - 1, h, j] = res[first:first + toks]

    def offset(block_z, i):
        return plan_ref[offs + i * n + 2 * block_z + y]

    def attend_block(t, h, block_z, first, sources):
        attend(
            t, h, kv[block_z, t, h], (first, first + 1),
            (offset(block_z, 0), offset(block_z, 1)), sources,
        )

    def r_near(t):
        return remote(
            ro.at[t, 0, :, 0:4], bk.at[t, :, pl.ds(y * 10, 4)], r_send.at[0, t], r_recv.at[0, t], mate
        )

    def r_early(src, t):
        who, kind = ((mate, 1), (end_own, 1), (end_mate, 2))[src]
        return remote(
            ro.at[t, src, :, 4:6], bk.at[t, :, pl.ds(y * 10 + 4, 2)], r_send.at[1 + src, t],
            r_recv.at[kind, t], who,
        )

    def r_late(src, t, h):
        who, kind = ((mate, 0), (end_own, 0), (end_mate, 1))[src]
        return remote(
            ro.at[t, src, h, 6:10], bk.at[t, h, pl.ds(y * 10 + 6, 4)], r_send.at[4 + 2 * src + h, t],
            r_recv.at[3 + 2 * kind + h, t], who,
        )

    def r_wait(part, sem, t):
        remote(part, part, r_send.at[0, t], r_recv.at[sem, t], mate).wait_recv()

    def r_wait_far(kind, column, t):
        r_wait(bk.at[t, :, pl.ds(column * 10 + 4, 2)], 1 + kind, t)
        for h in range(heads):
            r_wait(bk.at[t, h, pl.ds(column * 10 + 6, 4)], 3 + 2 * kind + h, t)

    def attend_near(t):
        @pl.when(is_end)
        def _():
            for h in range(heads):
                kv_wait(hub_z, t, h)

        @pl.when(is_hub)
        def _():
            q_near(t).wait_recv()

        for h in range(heads):
            attend_block(t, h, hub_z, 0, 2)
            attend_block(t, h, end_z, 2, 2)
        r_near(t).start()

    def attend_far(t):
        q_along(t).wait_recv()
        for h in range(heads):
            kv_wait(3 - hub_z, t, h)
            attend_block(t, h, 3 - hub_z, 4, 4)
        for src in range(3):
            r_early(src, t).start()
        hot = plan_ref[offs + 2 * n + 2]
        for h in range(heads):
            kv_wait(3 - end_z, t, h)
            attend_block(t, h, 3 - end_z, 6, 4)
            key = kv[0, t, h]
            for block_z in range(1, 4):
                key = jnp.where(hot == block_z, kv[block_z, t, h], key)
            attend(t, h, key, (8, 9), (plan_ref[offs + 2 * n], plan_ref[offs + 2 * n + 1]), 4)
            for src in range(3):
                r_late(src, t, h).start()

    def gather(t):
        r_wait(bk.at[t, :, pl.ds((1 - y) * 10, 4)], 0, t)

        @pl.when(is_hub)
        def _():
            r_wait_far(0, 1 - y, t)

        @pl.when(is_end)
        def _():
            r_wait_far(0, y, t)
            r_wait_far(1, 1 - y, t)

        cur[...] = bk[t]

        def pick(w, carry):
            for h in range(heads):
                cols = pl.ds(pl.multiple_of(t * wide + h * HEAD_DIM, HEAD_DIM), HEAD_DIM)
                attended[w, :, cols] = cur[h, plan_ref[spots + w]]
            return carry

        lax.fori_loop(0, windows, pick, 0)

    ahead = min(3, tiles)
    make_halo(jnp.int32(0))
    for copy in tables:
        copy.wait()
    fc, fs = mix_late(jnp.int32(0))
    for t in range(1, ahead):
        make_halo(jnp.int32(t))

    @pl.when(me == 0)
    def _():
        halo[...] = jnp.zeros_like(halo)

    pl.semaphore_wait(barrier, 3 + jnp.where(is_hub, 1, 0) + jnp.where(crosses, 1, 0))
    for t in range(ahead):
        send_halo(jnp.int32(t))
    mix_early(jnp.int32(0), fc, fs, True)
    hub_route(n, rows, blocks_ref, sites_ref, plan_ref)
    x_copy.wait()
    stage(jnp.int32(0))

    @pl.when(ahead < tiles)
    def _():
        make_halo(jnp.int32(min(ahead, tiles - 1)))
        send_halo(jnp.int32(min(ahead, tiles - 1)))
        pass_halo(jnp.int32(min(ahead, tiles - 1)))

    def step(s, carry):
        @pl.when(s + ahead < tiles)
        def _():
            make_halo(s + ahead)
            send_halo(s + ahead)

        @pl.when(s < tiles)
        def _():
            mix_early(s, *mix_late(s), False)
            stage(s)

        @pl.when(s + ahead < tiles)
        def _():
            pass_halo(s + ahead)

        @pl.when((s <= tiles) & is_end)
        def _():
            q_near(s - 1).wait_recv()
            q_along(s - 1).start()

        @pl.when((s >= 2) & (s <= tiles + 1))
        def _():
            attend_near(s - 2)

        @pl.when((s <= tiles) & is_hub)
        def _():
            forward(s - 1)

        @pl.when((s >= 2) & (s <= tiles + 1) & is_hub)
        def _():
            attend_far(s - 2)

        @pl.when(s >= 3)
        def _():
            gather(s - 3)

        return carry

    lax.fori_loop(1, tiles + 3, step, 0)

    def drain(t, carry):
        @pl.when(me < n - 1)
        def _():
            halo_copy(t).wait_send()

        @pl.when((y == 0) & (z < 3) & detour(t))
        def _():
            relay_on(t).wait_send()

        q_near(t).wait_send()
        r_near(t).wait_send()

        @pl.when(is_hub)
        def _():
            for h in range(heads):
                for which in range(3):
                    kv_copy(which, t, h).wait_send()
                for src in range(3):
                    r_late(src, t, h).wait_send()
            for src in range(3):
                r_early(src, t).wait_send()

        @pl.when(is_end)
        def _():
            for h in range(heads):
                kv_copy(3, t, h).wait_send()
            q_along(t).wait_send()

        for h in range(heads):
            hyena_copy(t, h).wait()
        return carry

    lax.fori_loop(0, tiles, drain, 0)


def settle_body(a_ref, b_ref, a_out, b_out, sems):
    copies = []
    for i, (src, dst) in enumerate(((a_ref, a_out), (b_ref, b_out))):
        part = src.shape[0] // 4
        for j in range(4):
            at = pl.ds(j * part, part)
            copies.append(pltpu.make_async_copy(src.at[at], dst.at[at], sems.at[i, j]))
    for copy in copies:
        copy.start()
    for copy in copies:
        copy.wait()


def settle(hyena, attended):
    anywhere = pl.BlockSpec(memory_space=pl.ANY)
    return pl.pallas_call(
        settle_body,
        out_shape=[jax.ShapeDtypeStruct(a.shape, a.dtype) for a in (hyena, attended)],
        in_specs=[pl.BlockSpec(memory_space=pltpu.VMEM)] * 2,
        out_specs=[anywhere] * 2,
        scratch_shapes=[pltpu.SemaphoreType.DMA((2, 4))],
        compiler_params=pltpu.CompilerParams(vmem_limit_bytes=16 * 1024 * 1024),
        name="settle",
    )(hyena, attended)


def hub(blocks, sites, temps, streams, filters, queries):
    gate, keys, values = streams
    rows, chans = gate.shape
    taps = filters.shape[1]
    windows, toks, _ = queries.shape
    wide = 2 * HEAD_DIM
    tiles = chans // wide
    half = jnp.bfloat16
    full = lambda *shape: pltpu.VMEM(shape, half)
    dma = lambda *shape: pltpu.SemaphoreType.DMA(shape)
    anywhere = pl.BlockSpec(memory_space=pl.ANY)
    return pl.pallas_call(
        hub_body,
        out_shape=[
            pltpu.VMEM((rows, chans), half),
            pltpu.VMEM((windows, toks, chans), half),
        ],
        in_specs=[pl.BlockSpec(memory_space=pltpu.SMEM)] * 3
        + [anywhere] * 8,
        out_specs=[pl.BlockSpec(memory_space=pltpu.VMEM)] * 2,
        scratch_shapes=[
            pltpu.SMEM((64,), jnp.int32),
            full(2 * taps, 2 * taps), full(2 * taps, 2 * taps), full(taps, 2 * taps),
            full(tiles, rows, wide), full(tiles, rows, wide), full(tiles, rows, wide),
            pltpu.VMEM((tiles, wide, taps), jnp.float32),
            full(windows, toks, chans),
            full(tiles, taps, wide), full(tiles, taps, wide), full(tiles, taps, wide),
            full(4, tiles, 2, rows, HEAD_DIM),
            full(tiles, 4, 10, toks, wide), full(tiles, 10, toks, wide),
            full(tiles, 3, 2, 10, toks, HEAD_DIM), full(tiles, 2, 20, toks, HEAD_DIM),
            full(2, 20, toks, HEAD_DIM),
            dma(4, tiles), dma(), dma(tiles), dma(tiles), dma(tiles), dma(tiles),
            dma(3, 2, tiles), dma(4, 2, tiles), dma(2, tiles), dma(2, tiles),
            dma(10, tiles), dma(7, tiles), dma(2, tiles), dma(3),
        ],
        compiler_params=pltpu.CompilerParams(
            collective_id=1, has_side_effects=True, vmem_limit_bytes=67043328 - 2 * chans * (rows + windows * toks)
        ),
        name="hub",
    )(blocks, sites, temps, *transforms(taps), gate, keys, values, filters, queries)


def shards(gate_stream, key_stream, value_stream, filters, temps, queries, blocks, sites):
    count = lax.axis_size("pos")
    streams = (gate_stream, key_stream, value_stream)
    if count == 8 and queries.shape[1] % 16 == 0:
        return tuple(settle(*hub(blocks, sites, temps, streams, filters, queries)))
    plan = route(blocks, sites, count, gate_stream.shape[0])
    return tuple(
        fused(plan, temps, streams, filters, queries, count)
    )


def solution(mesh):
    placed = (
        P(("groups", "pos"), "mp"),
        P(("groups", "pos"), "mp"),
        P(("groups", "pos"), "mp"),
        P("mp", None),
        P("mp"),
        P("groups", "pos", "mp"),
        P("groups"),
        P("groups"),
    )
    return jax.shard_map(
        shards,
        mesh=mesh,
        in_specs=placed,
        out_specs=(P(("groups", "pos"), "mp"), P("groups", "pos", "mp")),
        check_vma=False,
    )
```

```python
import functools
import math

import jax
import jax.numpy as jnp
import numpy as np
from jax import lax
from jax.experimental import pallas as pl
from jax.experimental.pallas import tpu as pltpu
from jax.sharding import PartitionSpec as P

HEAD_DIM = 128
LOG2E = math.log2(math.e)


def transforms(taps):
    size = 2 * taps
    freq = (np.arange(taps) + 0.5) * (2 * np.pi / size)
    grid = freq[:, None] * np.arange(size)[None, :]
    both = np.concatenate([np.cos(grid), np.sin(grid)], 0)
    forward = both / size
    short = both[:, :taps] / taps
    inverse = both[:, taps:].T * taps * 2.0
    cast = lambda a: jnp.asarray(a, jnp.bfloat16)
    return cast(forward), cast(np.concatenate([short, short], 1)), cast(inverse)


def unit(block):
    return block * lax.rsqrt(jnp.mean(block * block, axis=-1, keepdims=True) + 1e-06)


def route_body(n, rows, blocks_ref, sites_ref, o_ref, seen):
    windows = blocks_ref.shape[0]
    me = lax.axis_index("pos")
    info = 2 * n + 2 + windows

    def clear(i, carry):
        o_ref[i] = 0
        return carry

    def fresh(i, carry):
        seen[i] = 0
        return carry

    def one(w, carry):
        block = blocks_ref[w]
        within = seen[block]
        seen[block] = within + 1
        place = jnp.where(within < 2, within * n + block, 2 * n + within - 2)
        o_ref[place] = w
        o_ref[2 * n + 2 + w] = place
        mine = block == me
        o_ref[info + within] = jnp.where(mine, sites_ref[w] - me * rows, o_ref[info + within])
        o_ref[info + 4] = jnp.where(mine & (within == 2), 1, o_ref[info + 4])
        return carry

    lax.fori_loop(0, 2 * n + 2, clear, 0)
    lax.fori_loop(0, n, fresh, 0)
    for slot in range(4):
        o_ref[info + slot] = rows
    o_ref[info + 4] = 0
    lax.fori_loop(0, windows, one, 0)


def route(blocks, sites, n, rows):
    windows = blocks.shape[0]
    smem = pl.BlockSpec(memory_space=pltpu.SMEM)
    return pl.pallas_call(
        functools.partial(route_body, n, rows),
        out_shape=jax.ShapeDtypeStruct((2 * n + windows + 7,), jnp.int32),
        in_specs=[smem, smem],
        out_specs=smem,
        scratch_shapes=[pltpu.SMEM((n,), jnp.int32)],
        name="route",
    )(blocks, sites)


def fused_body(
    n, inner, plan_ref, temps_ref, fwd_ref, short_ref, inv_ref, g_hbm, k_hbm, v_hbm, f_hbm,
    x_hbm, hyena_out, out_ref,
    gv, kv, vv, fv, qv, s0, s1, tail, halo, hy, keyed, q0, q1, qx, o0, o1, ox, acc, side, rise,
    fall, back,
    load, local, halo_sem, go_send, go_recv, ret_send, ret_recv, up_send, up_recv,
    down_send, down_recv, part_send, part_recv, rpart_send, rpart_recv,
    rup_send, rup_recv, rdown_send, rdown_recv,
):
    outer = n // inner
    me = lax.axis_index("pos")
    zi, yi = me // inner, me % inner
    rows, chans = gv.shape
    taps = fv.shape[1]
    toks = q0.shape[1]
    wide = 2 * HEAD_DIM
    windows = qv.shape[0]
    info = 2 * n + 2 + windows

    def remote(src, dst, send, recv, who):
        return pltpu.make_async_remote_copy(
            src_ref=src, dst_ref=dst, send_sem=send, recv_sem=recv,
            device_id={"pos": who}, device_id_type=pl.DeviceIdType.MESH,
        )

    loads = [
        pltpu.make_async_copy(src, dst, load.at[i])
        for i, (src, dst) in enumerate(
            ((k_hbm, kv), (v_hbm, vv), (x_hbm, qv), (g_hbm, gv), (f_hbm, fv))
        )
    ]
    for copy in loads:
        copy.start()

    def norm(slot, dst, at, first):
        w = plan_ref[slot]
        for h in range(chans // HEAD_DIM):
            cols = slice(h * HEAD_DIM, (h + 1) * HEAD_DIM)
            dst[at, first:first + toks, cols] = unit(
                qv[w, :, cols].astype(jnp.float32)
            ).astype(jnp.bfloat16)

    barrier = pltpu.get_barrier_semaphore()
    for off in range(1, n):
        pl.semaphore_signal(
            barrier, inc=1, device_id={"pos": (me + off) % n}, device_id_type=pl.DeviceIdType.MESH
        )
    pl.semaphore_wait(barrier, n - 1)

    loads[0].wait()
    loads[1].wait()
    at = slice(rows - taps, rows)
    tail[...] = (kv[at].astype(jnp.float32) * vv[at].astype(jnp.float32)).astype(jnp.bfloat16)
    halo_copy = remote(tail, halo, halo_sem.at[0], halo_sem.at[1], (me + 1) % n)

    loads[2].wait()
    norm(2 * n, qx, me, 0)
    norm(2 * n + 1, qx, me, toks)

    def across(z):
        slot = z * inner + yi
        return remote(
            qx.at[slot], qx.at[slot], part_send.at[z], part_recv.at[z], zi * inner + (inner - 1 - yi)
        )

    def upward(step):
        slot = jnp.maximum(zi - step + 1, 0) * inner + yi
        to = jnp.minimum(zi + 1, outer - 1) * inner + yi
        return remote(qx.at[slot], qx.at[slot], up_send.at[step], up_recv.at[step], to)

    def downward(step):
        slot = jnp.minimum(zi + step - 1, outer - 1) * inner + yi
        to = jnp.maximum(zi - 1, 0) * inner + yi
        return remote(qx.at[slot], qx.at[slot], down_send.at[step], down_recv.at[step], to)

    def gather_send(step):
        @pl.when((zi >= step - 1) & (zi < outer - 1))
        def _():
            upward(step).start()

        @pl.when((zi + step - 1 < outer) & (zi > 0))
        def _():
            downward(step).start()

        if inner == 2:
            @pl.when(zi >= step - 1)
            def _():
                across(jnp.maximum(zi - step + 1, 0)).start()

            if step > 1:
                @pl.when(zi + step - 1 < outer)
                def _():
                    across(jnp.minimum(zi + step - 1, outer - 1)).start()

    def gather_recv(step):
        @pl.when(zi >= step)
        def _():
            upward(step).wait_recv()

        @pl.when(zi + step < outer)
        def _():
            downward(step).wait_recv()

    def out_copy(slot, src, dst, off):
        to = (me + off) % n
        return remote(src.at[to], dst.at[me], go_send.at[slot, off], go_recv.at[slot, off], to)

    def back_copy(slot, src, off):
        to = (me + off) % n
        return remote(src.at[to], back.at[slot * n + me], ret_send.at[slot, off], ret_recv.at[slot, off], to)

    gather_send(1)

    def send(slot, buf, dst, low, high):
        def one(off, carry):
            to = (me + off) % n
            norm(slot * n + to, buf, to, 0)
            out_copy(slot, buf, dst, off).start()
            return carry

        lax.fori_loop(low, high, one, 0)

    hops = max(outer - 1, 1)
    cuts = [1 + (n - 1) * i // hops for i in range(hops + 1)]
    for step in range(hops):
        send(0, s0, q0, cuts[step], cuts[step + 1])
        if step == 0:
            @pl.when(me < n - 1)
            def _():
                halo_copy.start()

        if outer > 1:
            gather_recv(step + 1)
            gather_send(step + 2)
    send(1, s1, q1, 1, n)
    norm(me, q0, me, 0)
    norm(n + me, q1, me, 0)

    loads[3].wait()
    loads[4].wait()

    @pl.when(me > 0)
    def _():
        halo_copy.wait_recv()

    @pl.when(me == 0)
    def _():
        halo[...] = jnp.zeros_like(halo)

    def mix_tile(c, carry):
        cols = pl.ds(pl.multiple_of(c * wide, wide), wide)
        filt = fv[cols, :]
        high = filt.astype(jnp.bfloat16)
        low = (filt - high.astype(jnp.float32)).astype(jnp.bfloat16)
        fhat = lax.dot_general(
            short_ref[...], jnp.concatenate([high, low], 1), (((1,), (1,)), ((), ())),
            preferred_element_type=jnp.float32,
        )
        fc, fs = fhat[:taps], fhat[taps:]
        before = halo[:, cols]
        for b in range(rows // taps):
            here = slice(b * taps, (b + 1) * taps)
            z = (kv[here, cols].astype(jnp.float32) * vv[here, cols].astype(jnp.float32)).astype(jnp.bfloat16)
            zhat = jnp.dot(
                fwd_ref[...], jnp.concatenate([before, z], 0), preferred_element_type=jnp.float32
            )
            before = z
            zc, zs = zhat[:taps], zhat[taps:]
            prod = jnp.concatenate(
                [(fc * zc - fs * zs).astype(jnp.bfloat16), (fc * zs + fs * zc).astype(jnp.bfloat16)], 0
            )
            mixed = jnp.dot(inv_ref[...], prod, preferred_element_type=jnp.float32)
            out = (gv[here, cols].astype(jnp.float32) * mixed).astype(jnp.bfloat16)
            hy[here, cols] = out
            out = out.astype(jnp.float32)
            keyed[here, cols] = jnp.concatenate(
                [unit(out[:, :HEAD_DIM]), unit(out[:, HEAD_DIM:])], 1
            ).astype(jnp.bfloat16)
        return carry

    tiles = chans // wide
    lax.fori_loop(0, tiles, mix_tile, 0)
    hyena_copy = pltpu.make_async_copy(hy, hyena_out, local.at[2])
    hyena_copy.start()


    def attend(slot, q, o, first, hot):
        off = plan_ref[info + slot]
        seen = off * hot

        def one(c, carry):
            place = lax.broadcasted_iota(jnp.int32, (rows, HEAD_DIM), 0)
            ones = jnp.where(place < off, 1.0, 0.0).astype(jnp.bfloat16)
            live = jnp.where(place < seen, 1.0, 0.0).astype(jnp.bfloat16)
            for half in range(2):
                cols = pl.ds(pl.multiple_of(c * wide + half * HEAD_DIM, HEAD_DIM), HEAD_DIM)
                rows_q = q[:, pl.ds(first, toks), cols]
                if toks % 16:
                    rows_q = rows_q.astype(jnp.float32)
                rows_q = rows_q.reshape(n * toks, HEAD_DIM).astype(jnp.bfloat16)
                valued = jnp.concatenate([hy[:, cols] * live, ones], 1)
                scores = lax.dot_general(
                    rows_q, keyed[:, cols], (((1,), (1,)), ((), ())),
                    preferred_element_type=jnp.float32,
                )
                weights = jnp.exp2(scores * (temps_ref[c * 2 + half] * (LOG2E / HEAD_DIM)))
                numer = jnp.dot(
                    weights.astype(jnp.bfloat16), valued, preferred_element_type=jnp.float32
                )
                res = numer[:, :HEAD_DIM] / numer[:, HEAD_DIM:]
                o[:, pl.ds(first, toks), cols] = res.reshape(n, toks, HEAD_DIM).astype(jnp.bfloat16)
            return carry

        lax.fori_loop(0, tiles, one, 0)

    if inner == 2:
        for z in range(outer):
            across(z).wait_recv()
    hot = plan_ref[info + 4]
    attend(2, qx, ox, 0, hot)
    attend(3, qx, ox, toks, hot)

    def swap(z):
        return remote(
            ox.at[z * inner + (inner - 1 - yi)], side.at[z], rpart_send.at[z], rpart_recv.at[z],
            zi * inner + (inner - 1 - yi),
        )

    if inner == 2:
        for z in range(outer):
            swap(z).start()

    for off in range(1, n):
        out_copy(0, s0, q0, off).wait_recv()
    attend(0, q0, o0, 0, 1)
    mine0 = pltpu.make_async_copy(o0.at[me], back.at[me], local.at[0])
    mine0.start()

    def lift(z):
        to = jnp.minimum(zi + 1, outer - 1) * inner + yi
        return remote(acc.at[z], rise.at[z], rup_send.at[z], rup_recv.at[z], to)

    def drop(z):
        to = jnp.maximum(zi - 1, 0) * inner + yi
        return remote(acc.at[z], fall.at[z], rdown_send.at[z], rdown_recv.at[z], to)

    for z in range(outer):
        if inner == 2:
            swap(z).wait_recv()
            acc[z] = ox[z * inner + yi] + side[z]
        else:
            acc[z] = ox[z]

    def reduce_up(z):
        @pl.when(zi < z)
        def _():
            @pl.when(zi > 0)
            def _():
                lift(z).wait_recv()
                acc[z] = acc[z] + rise[z]

            lift(z).start()

    def reduce_down(z):
        @pl.when(zi > z)
        def _():
            @pl.when(zi < outer - 1)
            def _():
                drop(z).wait_recv()
                acc[z] = acc[z] + fall[z]

            drop(z).start()

    def reduce(step):
        if outer > 1:
            reduce_up(outer - 1 - step)
            reduce_down(step)

    reduce(0)
    for off in range(1, n):
        back_copy(0, o0, off).start()
    for off in range(1, n):
        out_copy(1, s1, q1, off).wait_recv()
    attend(1, q1, o1, 0, 1)
    mine1 = pltpu.make_async_copy(o1.at[me], back.at[n + me], local.at[1])
    mine1.start()
    rest = max(hops - 1, 1)
    cuts = [1 + (n - 1) * i // rest for i in range(rest + 1)]
    for step in range(rest):
        if step + 1 < hops:
            reduce(step + 1)
        for off in range(cuts[step], cuts[step + 1]):
            back_copy(1, o1, off).start()
    back[2 * n] = acc[zi, :toks]
    back[2 * n + 1] = acc[zi, toks:]

    def add(ref):
        back[2 * n] = back[2 * n] + ref[zi, :toks]
        back[2 * n + 1] = back[2 * n + 1] + ref[zi, toks:]

    @pl.when(zi > 0)
    def _():
        lift(zi).wait_recv()
        add(rise)

    @pl.when(zi < outer - 1)
    def _():
        drop(zi).wait_recv()
        add(fall)

    mine0.wait()
    mine1.wait()
    for off in range(1, n):
        back_copy(0, o0, off).wait_recv()
        back_copy(1, o1, off).wait_recv()

    def pick(w, carry):
        out_ref[w] = back[plan_ref[2 * n + 2 + w]]
        return carry

    lax.fori_loop(0, windows, pick, 0)

    for off in range(1, n):
        out_copy(0, s0, q0, off).wait_send()
        out_copy(1, s1, q1, off).wait_send()
        back_copy(0, o0, off).wait_send()
        back_copy(1, o1, off).wait_send()

    @pl.when(me < n - 1)
    def _():
        halo_copy.wait_send()

    for step in range(1, outer):
        @pl.when((zi >= step - 1) & (zi < outer - 1))
        def _(step=step):
            upward(step).wait_send()

        @pl.when((zi + step - 1 < outer) & (zi > 0))
        def _(step=step):
            downward(step).wait_send()

    for z in range(outer):
        if inner == 2:
            across(z).wait_send()
            swap(z).wait_send()

        @pl.when(zi < z)
        def _(z=z):
            lift(z).wait_send()

        @pl.when(zi > z)
        def _(z=z):
            drop(z).wait_send()

    hyena_copy.wait()


def fused(plan, temps, streams, filters, queries, n):
    gate, keys, values = streams
    rows, chans = gate.shape
    taps = filters.shape[1]
    windows, toks, _ = queries.shape
    inner = 2 if n % 2 == 0 else 1
    outer = n // inner
    half = jnp.bfloat16
    full = lambda *shape: pltpu.VMEM(shape, half)
    dma = lambda *shape: pltpu.SemaphoreType.DMA(shape)
    anywhere = pl.BlockSpec(memory_space=pl.ANY)
    return pl.pallas_call(
        functools.partial(fused_body, n, inner),
        out_shape=[
            jax.ShapeDtypeStruct((rows, chans), half),
            jax.ShapeDtypeStruct((windows, toks, chans), half),
        ],
        in_specs=[pl.BlockSpec(memory_space=pltpu.SMEM)] * 2
        + [pl.BlockSpec(memory_space=pltpu.VMEM)] * 3
        + [anywhere] * 5,
        out_specs=[anywhere, pl.BlockSpec(memory_space=pltpu.VMEM)],
        scratch_shapes=[
            full(rows, chans), full(rows, chans), full(rows, chans),
            pltpu.VMEM((chans, taps), jnp.float32),
            full(windows, toks, chans), full(n, toks, chans), full(n, toks, chans),
            full(taps, chans), full(taps, chans), full(rows, chans), full(rows, chans),
            full(n, toks, chans), full(n, toks, chans), full(n, 2 * toks, chans),
            full(n, toks, chans), full(n, toks, chans), full(n, 2 * toks, chans),
            full(outer, 2 * toks, chans), full(outer, 2 * toks, chans),
            full(outer, 2 * toks, chans), full(outer, 2 * toks, chans),
            full(2 * n + 2, toks, chans),
            dma(5), dma(3), dma(2), dma(2, n), dma(2, n), dma(2, n), dma(2, n),
            dma(outer + 1), dma(outer + 1), dma(outer + 1), dma(outer + 1),
            dma(outer), dma(outer), dma(outer), dma(outer),
            dma(outer), dma(outer), dma(outer), dma(outer),
        ],
        compiler_params=pltpu.CompilerParams(
            collective_id=0, has_side_effects=True, vmem_limit_bytes=67043328
        ),
        name="fused",
    )(plan, temps, *transforms(taps), gate, keys, values, filters, queries)


def hub_route(n, rows, blocks_ref, sites_ref, plan_ref):
    windows = blocks_ref.shape[0]
    half = lax.axis_index("pos") // 4
    spots, offs = 2 * n + 2, 2 * n + 2 + windows
    blocks = [jnp.clip(blocks_ref[w], 0, n - 1) for w in range(windows)]
    places = []
    hot = jnp.int32(0)
    for w, block in enumerate(blocks):
        within = jnp.int32(0)
        for other in blocks[:w]:
            within = within + jnp.where(other == block, 1, 0)
        within = jnp.minimum(within, 3)
        places.append(jnp.where(within < 2, within * n + block, 2 * n + within - 2))
        z = lax.shift_right_logical(block, 1)
        far = jnp.where((z >= 2) == (half == 1), 0, 4)
        at_end = jnp.where((z == 0) | (z == 3), 2, 0)
        slot = jnp.where(within < 2, far + at_end + within, 6 + within)
        plan_ref[spots + w] = (block - 2 * z) * 10 + slot
        hot = jnp.where(within >= 2, z, hot)
    plan_ref[offs + 2 * n + 2] = hot
    reach = [sites_ref[w] - blocks[w] * rows for w in range(windows)]
    for p in range(2 * n + 2):
        w, off = jnp.int32(0), jnp.int32(0)
        for v in range(windows):
            hit = places[v] == p
            w = jnp.where(hit, v, w)
            off = jnp.where(hit, reach[v], off)
        plan_ref[p] = w
        plan_ref[offs + p] = off


def hub_body(
    blocks_ref, sites_ref, temps_ref, fwd_hbm, short_hbm, inv_hbm, g_hbm, k_hbm, v_hbm, f_hbm, x_hbm,
    hyena_out, attended,
    plan_ref, fwd_ref, short_ref, inv_ref, kt, vt, gt, ft, qv, tail, relay, halo, kv, qr, qs, ro, bk, cur,
    load, x_sem, halo_send, halo_recv, relay_send, relay_recv, kv_send, kv_recv, q_send, q_recv,
    r_send, r_recv, hy_sem, table_sem,
):
    n = 8
    tiles, rows, wide = kt.shape
    heads = wide // HEAD_DIM
    taps = ft.shape[2]
    windows, toks, _ = qv.shape
    me = lax.axis_index("pos")
    z, y = me // 2, me % 2
    half = z // 2
    hub_z = 1 + half
    end_z = 3 * half
    is_hub = z == hub_z
    is_end = z == end_z
    mate = 2 * z + 1 - y
    hub_own, hub_mate = 2 * hub_z + y, 2 * hub_z + 1 - y
    end_own, end_mate = 2 * end_z + y, 2 * end_z + 1 - y
    twin = 2 * (3 - hub_z) + y
    spots, offs = 2 * n + 2, 2 * n + 2 + windows

    def remote(src, dst, send, recv, who):
        return pltpu.make_async_remote_copy(
            src_ref=src, dst_ref=dst, send_sem=send, recv_sem=recv,
            device_id={"pos": who}, device_id_type=pl.DeviceIdType.MESH,
        )

    def columns(t):
        return pl.ds(pl.multiple_of(t * wide, wide), wide)

    def loads(t, which):
        pairs = (
            (k_hbm.at[:, columns(t)], kt), (v_hbm.at[:, columns(t)], vt),
            (f_hbm.at[columns(t), :], ft), (g_hbm.at[:, columns(t)], gt),
        )
        return [pltpu.make_async_copy(pairs[i][0], pairs[i][1].at[t], load.at[i, t]) for i in which]

    def load_start(t, carry):
        for copy in loads(t, range(4)):
            copy.start()
        return carry

    barrier = pltpu.get_barrier_semaphore()

    def greet(who):
        pl.semaphore_signal(
            barrier, inc=1, device_id={"pos": who}, device_id_type=pl.DeviceIdType.MESH
        )

    crosses = (me == 3) | (me == 4)
    for off in range(1, 4):
        greet(4 * half + (me + off) % 4)

    @pl.when(is_hub)
    def _():
        greet(twin)

    @pl.when(crosses)
    def _():
        greet(7 - me)

    tables = [
        pltpu.make_async_copy(src, dst, table_sem.at[i])
        for i, (src, dst) in enumerate(((short_hbm, short_ref), (fwd_hbm, fwd_ref), (inv_hbm, inv_ref)))
    ]
    for copy in tables:
        copy.start()
    load_start(0, 0)
    x_copy = pltpu.make_async_copy(x_hbm, qv, x_sem)
    x_copy.start()
    lax.fori_loop(1, tiles, load_start, 0)

    def halo_copy(t):
        return remote(tail.at[t], halo.at[t], halo_send.at[t], halo_recv.at[t], (me + 1) % n)

    def relay_in(t):
        return remote(tail.at[t], relay.at[t], halo_send.at[t], relay_recv.at[t], mate)

    def relay_on(t):
        return remote(relay.at[t], halo.at[t], relay_send.at[t], halo_recv.at[t], (me + 2) % n)

    def detour(t):
        return t >= 4

    def make_halo(t):
        for copy in loads(t, (0, 1)):
            copy.wait()
        at = slice(rows - taps, rows)
        tail[t] = (kt[t, at].astype(jnp.float32) * vt[t, at].astype(jnp.float32)).astype(jnp.bfloat16)

    def send_halo(t):
        @pl.when((y == 0) | ((me < n - 1) & ~detour(t)))
        def _():
            halo_copy(t).start()

        @pl.when((y == 1) & (me < n - 1) & detour(t))
        def _():
            relay_in(t).start()

    def pass_halo(t):
        @pl.when((y == 0) & (z < 3) & detour(t))
        def _():
            relay_in(t).wait_recv()
            relay_on(t).start()

    whole = slice(0, rows)

    def kv_copy(which, t, h, at=whole):
        block, who = ((z, twin), (z, end_own), (end_z, twin), (z, hub_own))[which]
        part = kv.at[block, t, h, at]
        return remote(part, part, kv_send.at[which % 3, h, t], kv_recv.at[block, h, t], who)

    def kv_wait(block, t, h):
        part = kv.at[block, t, h]
        remote(part, part, kv_send.at[0, h, t], kv_recv.at[block, h, t], mate).wait_recv()

    def kv_start(t, at):
        @pl.when(is_hub)
        def _():
            for which in range(2):
                for h in range(heads):
                    kv_copy(which, t, h, at).start()

        @pl.when(is_end)
        def _():
            for h in range(heads):
                kv_copy(3, t, h, at).start()

    def hyena_copy(t, h):
        cols = pl.ds(pl.multiple_of(t * wide + h * HEAD_DIM, HEAD_DIM), HEAD_DIM)
        return pltpu.make_async_copy(kv.at[z, t, h], hyena_out.at[:, cols], hy_sem.at[h, t])

    def product(t, b):
        here = slice(b * taps, (b + 1) * taps)
        return (kt[t, here].astype(jnp.float32) * vt[t, here].astype(jnp.float32)).astype(jnp.bfloat16)

    def spectrum(t):
        filt = ft[t]
        high = filt.astype(jnp.bfloat16)
        low = (filt - high.astype(jnp.float32)).astype(jnp.bfloat16)
        fhat = lax.dot_general(
            short_ref[...], jnp.concatenate([high, low], 1), (((1,), (1,)), ((), ())),
            preferred_element_type=jnp.float32,
        )
        return fhat[:taps], fhat[taps:]

    def piece(t, b, before, prod, fc, fs):
        here = slice(b * taps, (b + 1) * taps)
        zhat = jnp.dot(
            fwd_ref[...], jnp.concatenate([before, prod], 0), preferred_element_type=jnp.float32
        )
        zc, zs = zhat[:taps], zhat[taps:]
        both = jnp.concatenate(
            [(fc * zc - fs * zs).astype(jnp.bfloat16), (fc * zs + fs * zc).astype(jnp.bfloat16)], 0
        )
        mixed = jnp.dot(inv_ref[...], both, preferred_element_type=jnp.float32)
        out = (gt[t, here].astype(jnp.float32) * mixed).astype(jnp.bfloat16)
        for h in range(heads):
            kv[z, t, h, here] = out[:, h * HEAD_DIM:(h + 1) * HEAD_DIM]

    def mix_late(t):
        for copy in loads(t, (2, 3)):
            copy.wait()
        fc, fs = spectrum(t)
        before = product(t, 0)
        for b in range(1, rows // taps):
            prod = product(t, b)
            piece(t, b, before, prod, fc, fs)
            before = prod
        return fc, fs

    def mix_early(t, fc, fs, split):
        if split:
            kv_start(t, slice(taps, rows))

        @pl.when(me > 0)
        def _():
            halo_copy(t).wait_recv()

        piece(t, 0, halo[t], product(t, 0), fc, fs)
        kv_start(t, slice(0, taps) if split else whole)
        for h in range(heads):
            hyena_copy(t, h).start()

    def forward(t):
        for h in range(heads):
            kv_wait(end_z, t, h)
            kv_copy(2, t, h).start()

    def q_near(t):
        return remote(qs.at[t], qr.at[t, 1], q_send.at[0, t], q_recv.at[0, t], mate)

    def q_along(t):
        return remote(
            qr.at[t, 0:2, 4:10], qr.at[t, 2:4, 4:10], q_send.at[1, t], q_recv.at[1, t], hub_own
        )

    def slot_z(j):
        return ((hub_z, end_z), (3 - hub_z, 3 - end_z))[j // 4][(j % 4) // 2]

    def stage(t):
        for j in range(10):
            for own in range(2):
                column = y if own else 1 - y
                if j < 8:
                    block = 2 * slot_z(j) + column
                    w = plan_ref[(j % 2) * n + block]
                else:
                    w = plan_ref[2 * n + j - 8]
                for h in range(wide // HEAD_DIM):
                    cols = pl.ds(pl.multiple_of(t * wide + h * HEAD_DIM, HEAD_DIM), HEAD_DIM)
                    got = unit(qv[w, :, cols].astype(jnp.float32)).astype(jnp.bfloat16)
                    put = slice(h * HEAD_DIM, (h + 1) * HEAD_DIM)
                    if own:
                        qr[t, 0, j, :, put] = got
                    else:
                        qs[t, j, :, put] = got
        q_near(t).start()

    def attend(t, h, key, slots, offsets, sources):
        lane = lax.broadcasted_iota(jnp.int32, (1, rows), 1)
        many = sources * toks
        cols = slice(h * HEAD_DIM, (h + 1) * HEAD_DIM)
        power = lax.dot_general(
            jnp.ones((8, HEAD_DIM), jnp.bfloat16), key * key, (((1,), (1,)), ((), ())),
            preferred_element_type=jnp.float32,
        )[:1]
        scale = lax.rsqrt(power * (1.0 / HEAD_DIM) + 1e-06) * (
            temps_ref[t * heads + h] * (LOG2E / HEAD_DIM)
        )
        query = jnp.concatenate(
            [qr[t, 0:sources, j, :, cols].reshape(many, HEAD_DIM) for j in slots], 0
        )
        scores = lax.dot_general(
            query, key, (((1,), (1,)), ((), ())), preferred_element_type=jnp.float32
        )
        raised = jnp.exp2(scores * scale)
        weights = jnp.concatenate(
            [
                jnp.where(lane < off, raised[i * many:(i + 1) * many], 0.0).astype(jnp.bfloat16)
                for i, off in enumerate(offsets)
            ], 0
        )
        numer = jnp.dot(
            weights, jnp.concatenate([key, jnp.ones((rows, HEAD_DIM), jnp.bfloat16)], 1),
            preferred_element_type=jnp.float32,
        )
        res = (numer[:, :HEAD_DIM] / numer[:, HEAD_DIM:]).astype(jnp.bfloat16)
        for i, j in enumerate(slots):
            for src in range(sources):
                first = (i * sources + src) * toks
                if src == 0:
                    bk[t, h, y * 10 + j] = res[first:first + toks]
                else:
                    ro[t, src - 1, h, j] = res[first:first + toks]

    def offset(block_z, i):
        return plan_ref[offs + i * n + 2 * block_z + y]

    def attend_block(t, h, block_z, first, sources):
        attend(
            t, h, kv[block_z, t, h], (first, first + 1),
            (offset(block_z, 0), offset(block_z, 1)), sources,
        )

    def r_near(t):
        return remote(
            ro.at[t, 0, :, 0:4], bk.at[t, :, pl.ds(y * 10, 4)], r_send.at[0, t], r_recv.at[0, t], mate
        )

    def r_early(src, t):
        who, kind = ((mate, 1), (end_own, 1), (end_mate, 2))[src]
        return remote(
            ro.at[t, src, :, 4:6], bk.at[t, :, pl.ds(y * 10 + 4, 2)], r_send.at[1 + src, t],
            r_recv.at[kind, t], who,
        )

    def r_late(src, t, h):
        who, kind = ((mate, 0), (end_own, 0), (end_mate, 1))[src]
        return remote(
            ro.at[t, src, h, 6:10], bk.at[t, h, pl.ds(y * 10 + 6, 4)], r_send.at[4 + 2 * src + h, t],
            r_recv.at[3 + 2 * kind + h, t], who,
        )

    def r_wait(part, sem, t):
        remote(part, part, r_send.at[0, t], r_recv.at[sem, t], mate).wait_recv()

    def r_wait_far(kind, column, t):
        r_wait(bk.at[t, :, pl.ds(column * 10 + 4, 2)], 1 + kind, t)
        for h in range(heads):
            r_wait(bk.at[t, h, pl.ds(column * 10 + 6, 4)], 3 + 2 * kind + h, t)

    def attend_near(t):
        @pl.when(is_end)
        def _():
            for h in range(heads):
                kv_wait(hub_z, t, h)

        @pl.when(is_hub)
        def _():
            q_near(t).wait_recv()

        for h in range(heads):
            attend_block(t, h, hub_z, 0, 2)
            attend_block(t, h, end_z, 2, 2)
        r_near(t).start()

    def attend_far(t):
        q_along(t).wait_recv()
        for h in range(heads):
            kv_wait(3 - hub_z, t, h)
            attend_block(t, h, 3 - hub_z, 4, 4)
        for src in range(3):
            r_early(src, t).start()
        hot = plan_ref[offs + 2 * n + 2]
        for h in range(heads):
            kv_wait(3 - end_z, t, h)
            attend_block(t, h, 3 - end_z, 6, 4)
            key = kv[0, t, h]
            for block_z in range(1, 4):
                key = jnp.where(hot == block_z, kv[block_z, t, h], key)
            attend(t, h, key, (8, 9), (plan_ref[offs + 2 * n], plan_ref[offs + 2 * n + 1]), 4)
            for src in range(3):
                r_late(src, t, h).start()

    def gather(t):
        r_wait(bk.at[t, :, pl.ds((1 - y) * 10, 4)], 0, t)

        @pl.when(is_hub)
        def _():
            r_wait_far(0, 1 - y, t)

        @pl.when(is_end)
        def _():
            r_wait_far(0, y, t)
            r_wait_far(1, 1 - y, t)

        cur[...] = bk[t]

        def pick(w, carry):
            for h in range(heads):
                cols = pl.ds(pl.multiple_of(t * wide + h * HEAD_DIM, HEAD_DIM), HEAD_DIM)
                attended[w, :, cols] = cur[h, plan_ref[spots + w]]
            return carry

        lax.fori_loop(0, windows, pick, 0)

    ahead = min(3, tiles)
    make_halo(jnp.int32(0))
    for copy in tables:
        copy.wait()
    fc, fs = mix_late(jnp.int32(0))
    for t in range(1, ahead):
        make_halo(jnp.int32(t))

    @pl.when(me == 0)
    def _():
        halo[...] = jnp.zeros_like(halo)

    pl.semaphore_wait(barrier, 3 + jnp.where(is_hub, 1, 0) + jnp.where(crosses, 1, 0))
    for t in range(ahead):
        send_halo(jnp.int32(t))
    mix_early(jnp.int32(0), fc, fs, True)
    hub_route(n, rows, blocks_ref, sites_ref, plan_ref)
    x_copy.wait()
    stage(jnp.int32(0))

    @pl.when(ahead < tiles)
    def _():
        make_halo(jnp.int32(min(ahead, tiles - 1)))
        send_halo(jnp.int32(min(ahead, tiles - 1)))
        pass_halo(jnp.int32(min(ahead, tiles - 1)))

    def step(s, carry):
        @pl.when(s + ahead < tiles)
        def _():
            make_halo(s + ahead)
            send_halo(s + ahead)

        @pl.when(s < tiles)
        def _():
            mix_early(s, *mix_late(s), False)
            stage(s)

        @pl.when((s <= tiles) & is_end)
        def _():
            q_near(s - 1).wait_recv()
            q_along(s - 1).start()

        @pl.when((s >= 2) & (s <= tiles + 1))
        def _():
            attend_near(s - 2)

        @pl.when((s <= tiles) & is_hub)
        def _():
            forward(s - 1)

        @pl.when(s + ahead < tiles)
        def _():
            pass_halo(s + ahead)

        @pl.when((s >= 2) & (s <= tiles + 1) & is_hub)
        def _():
            attend_far(s - 2)

        @pl.when(s >= 3)
        def _():
            gather(s - 3)

        return carry

    lax.fori_loop(1, tiles + 3, step, 0)

    def drain(t, carry):
        @pl.when(me < n - 1)
        def _():
            halo_copy(t).wait_send()

        @pl.when((y == 0) & (z < 3) & detour(t))
        def _():
            relay_on(t).wait_send()

        q_near(t).wait_send()
        r_near(t).wait_send()

        @pl.when(is_hub)
        def _():
            for h in range(heads):
                for which in range(3):
                    kv_copy(which, t, h).wait_send()
                for src in range(3):
                    r_late(src, t, h).wait_send()
            for src in range(3):
                r_early(src, t).wait_send()

        @pl.when(is_end)
        def _():
            for h in range(heads):
                kv_copy(3, t, h).wait_send()
            q_along(t).wait_send()

        for h in range(heads):
            hyena_copy(t, h).wait()
        return carry

    lax.fori_loop(0, tiles, drain, 0)


def settle_body(a_ref, b_ref, a_out, b_out, sems):
    copies = []
    for i, (src, dst) in enumerate(((a_ref, a_out), (b_ref, b_out))):
        part = src.shape[0] // 4
        for j in range(4):
            at = pl.ds(j * part, part)
            copies.append(pltpu.make_async_copy(src.at[at], dst.at[at], sems.at[i, j]))
    for copy in copies:
        copy.start()
    for copy in copies:
        copy.wait()


def settle(hyena, attended):
    anywhere = pl.BlockSpec(memory_space=pl.ANY)
    return pl.pallas_call(
        settle_body,
        out_shape=[jax.ShapeDtypeStruct(a.shape, a.dtype) for a in (hyena, attended)],
        in_specs=[pl.BlockSpec(memory_space=pltpu.VMEM)] * 2,
        out_specs=[anywhere] * 2,
        scratch_shapes=[pltpu.SemaphoreType.DMA((2, 4))],
        compiler_params=pltpu.CompilerParams(vmem_limit_bytes=16 * 1024 * 1024),
        name="settle",
    )(hyena, attended)


def hub(blocks, sites, temps, streams, filters, queries):
    gate, keys, values = streams
    rows, chans = gate.shape
    taps = filters.shape[1]
    windows, toks, _ = queries.shape
    wide = 2 * HEAD_DIM
    tiles = chans // wide
    half = jnp.bfloat16
    full = lambda *shape: pltpu.VMEM(shape, half)
    dma = lambda *shape: pltpu.SemaphoreType.DMA(shape)
    anywhere = pl.BlockSpec(memory_space=pl.ANY)
    return pl.pallas_call(
        hub_body,
        out_shape=[
            pltpu.VMEM((rows, chans), half),
            pltpu.VMEM((windows, toks, chans), half),
        ],
        in_specs=[pl.BlockSpec(memory_space=pltpu.SMEM)] * 3
        + [anywhere] * 8,
        out_specs=[pl.BlockSpec(memory_space=pltpu.VMEM)] * 2,
        scratch_shapes=[
            pltpu.SMEM((64,), jnp.int32),
            full(2 * taps, 2 * taps), full(2 * taps, 2 * taps), full(taps, 2 * taps),
            full(tiles, rows, wide), full(tiles, rows, wide), full(tiles, rows, wide),
            pltpu.VMEM((tiles, wide, taps), jnp.float32),
            full(windows, toks, chans),
            full(tiles, taps, wide), full(tiles, taps, wide), full(tiles, taps, wide),
            full(4, tiles, 2, rows, HEAD_DIM),
            full(tiles, 4, 10, toks, wide), full(tiles, 10, toks, wide),
            full(tiles, 3, 2, 10, toks, HEAD_DIM), full(tiles, 2, 20, toks, HEAD_DIM),
            full(2, 20, toks, HEAD_DIM),
            dma(4, tiles), dma(), dma(tiles), dma(tiles), dma(tiles), dma(tiles),
            dma(3, 2, tiles), dma(4, 2, tiles), dma(2, tiles), dma(2, tiles),
            dma(10, tiles), dma(7, tiles), dma(2, tiles), dma(3),
        ],
        compiler_params=pltpu.CompilerParams(
            collective_id=1, has_side_effects=True, vmem_limit_bytes=67043328 - 2 * chans * (rows + windows * toks)
        ),
        name="hub",
    )(blocks, sites, temps, *transforms(taps), gate, keys, values, filters, queries)


def shards(gate_stream, key_stream, value_stream, filters, temps, queries, blocks, sites):
    count = lax.axis_size("pos")
    streams = (gate_stream, key_stream, value_stream)
    if count == 8 and queries.shape[1] % 16 == 0:
        return tuple(settle(*hub(blocks, sites, temps, streams, filters, queries)))
    plan = route(blocks, sites, count, gate_stream.shape[0])
    return tuple(
        fused(plan, temps, streams, filters, queries, count)
    )


def solution(mesh):
    placed = (
        P(("groups", "pos"), "mp"),
        P(("groups", "pos"), "mp"),
        P(("groups", "pos"), "mp"),
        P("mp", None),
        P("mp"),
        P("groups", "pos", "mp"),
        P("groups"),
        P("groups"),
    )
    return jax.shard_map(
        shards,
        mesh=mesh,
        in_specs=placed,
        out_specs=(P(("groups", "pos"), "mp"), P("groups", "pos", "mp")),
        check_vma=False,
    )
```
